512 devices in a mesh: pipe: 16 (over y, x_hi), expert: 32 (over z, x_lo, core).
Axes of the slice: x: 4 (x_hi: 2, x_lo: 2; x = x_hi * 2 + x_lo), y: 8, z: 8, core: 2. Of those that a mesh axis runs over, the one named last changes fastest.
Arguments:
- section_acts: bfloat16 [16, 2048, 2560], P('pipe', 'expert'), may hold values from -6 to 6
- section_grads: bfloat16 [16, 2048, 2560], P('pipe', 'expert'), may hold values from -6 to 6
- routes_fwd: int32 [16, 2048, 2], P('pipe', 'expert'), may hold values from 0 to 7, all different within a row; in each aligned block of 64 rows (0 to 63, 64 to 127, ..., all dimensions but the last counted through in order) at most 20 rows name the same one
- gate_fwd: int32 [16, 2048, 2], P('pipe', 'expert'), may hold values from 32 to 255
- routes_bwd: int32 [16, 2048, 2], P('pipe', 'expert'), may hold values from 0 to 7, all different within a row; in each aligned block of 64 rows (0 to 63, 64 to 127, ..., all dimensions but the last counted through in order) at most 20 rows name the same one
- gate_bwd: int32 [16, 2048, 2], P('pipe', 'expert'), may hold values from 32 to 255
- saved_pre: bfloat16 [16, 32, 32, 20, 384], P('pipe', 'expert'), may hold values from -6 to 6
- w_gate_up: bfloat16 [16, 32, 2560, 384], P('pipe', 'expert'), may hold values from -0.125 to 0.125
- w_down: bfloat16 [16, 32, 192, 2560], P('pipe', 'expert'), may hold values from -0.21875 to 0.21875
Outputs:
- moe_out: bfloat16 [16, 2048, 2560], P('pipe', 'expert')
- input_grad: bfloat16 [16, 2048, 2560], P('pipe', 'expert')
The draws below stay inside these ranges and needn't reach their ends.
Inputs may be any that keep to these rules, and one draw needn't show every extreme that they name: `routes_fwd`: among the tokens of one index of expert, no expert is named more than 20 times; in every draw some expert is named exactly 20 times by the tokens of some index. The 2 experts of a token differ. `routes_bwd`: among the tokens of one index of expert, no expert is named more than 20 times; in every draw some expert is named exactly 20 times by the tokens of some index. The 2 experts of a token differ.
All inputs are finite; a program needn't handle non-finite values.
Results may differ from the reference program's by a relative error of at most 0.0059.
Values may be sent and summed in bfloat16 or wider, within the bound.
A program may use at most 128 MiB of HBM per device.

```python
import math
import jax
import jax.numpy as jnp
import numpy as np
from jax import lax

D = 2560
H = 768
EXPERTS = 8
TOP = 2
TOK_DEV = 64
GROUP = 4
HID_DEV = 192
CAP = 20
TOKENS = 2048
SECTIONS = 16
BLOCKS = 32


def set_ends(array, stream_key, low, top_value):
    longest = array.shape.index(max(array.shape))
    spots = []
    for shift in (0, 1):
        where = [jax.random.randint(jax.random.fold_in(stream_key, axis), (), 0, length) for axis, length in enumerate(array.shape)]
        where[longest] = (where[longest] + shift) % array.shape[longest]
        spots.append(tuple(where))
    return array.at[spots[0]].set(low).at[spots[1]].set(top_value)


def level_of(own_key, shape, split, low, top_value):
    def one(position, parts):
        heights = jax.random.uniform(jax.random.fold_in(jax.random.fold_in(own_key, 6), position), (parts,), jnp.float32, low / len(split), top_value / len(split))
        return jnp.repeat(jnp.exp(heights), shape[position] // parts).reshape((-1,) + (1,) * (len(shape) - position - 1))

    level = one(*split[0])
    for cut in split[1:]:
        level = level * one(*cut)
    return level


def assign_block(rng, own, number, rows, number_of, top, reach, slope):
    ranking = jax.random.permutation(rng, number_of)
    packed, common = portions_of(number_of, rows * top, reach, slope, True), portions_of(number_of, rows * top, reach, slope, False)
    places = jnp.arange(number_of)

    def named(tallies, rotation):
        used = int((tallies > 0).sum())
        fixed = max(1, used // 4)
        moved = fixed + (places - fixed + rotation * (used - fixed)) % max(1, number_of - fixed)
        return jnp.zeros((number_of,), jnp.int32).at[ranking[jnp.where(places < fixed, places, moved)]].set(jnp.asarray(tallies, jnp.int32))

    tallies = jnp.where(number % 4 == 0, named(packed, number // 4), named(common, number - number // 4 - 1))
    mixed = jax.random.permutation(jax.random.fold_in(own, 3), number_of)
    source_of, receiver = mixed[0:number_of // 2 * 2:2], mixed[1:number_of // 2 * 2:2]
    margin = jnp.minimum(tallies[source_of] - 1, reach - tallies[receiver]) // 2
    margin = jnp.where((source_of == ranking[0]) | (receiver == ranking[0]) | (tallies[receiver] == 0), 0, jnp.maximum(margin, 0))
    moved = jax.random.randint(jax.random.fold_in(own, 4), (number_of // 2,), 0, 1 << 20) % (margin + 1)
    tallies = tallies.at[source_of].add(-moved).at[receiver].add(moved)
    members = jnp.searchsorted(jnp.cumsum(tallies), jnp.arange(rows * top), side="right").astype(jnp.int32)
    table = members.reshape(top, rows).T
    table = table[jax.random.permutation(jax.random.fold_in(own, 1), rows)]
    rotation = jax.random.randint(jax.random.fold_in(own, 2), (rows, 1), 0, top)
    return jnp.take_along_axis(table, (jnp.arange(top)[None, :] + rotation) % top, axis=1)


def portions_of(amount, total, reach, skew, full):
    weights = [(1 << 20) // math.isqrt(standing ** skew) + 1 for standing in range(1, amount + 1)]
    largest = reach if full else min(reach, max(-(-total // amount), total * weights[0] // sum(weights)))
    least = 1 if total - largest >= amount - 1 else 0
    counts, spare = [largest] + [least] * (amount - 1), total - largest - least * (amount - 1)
    while spare > 0:
        movable = [i for i in range(1, amount) if counts[i] < largest] or [i for i in range(1, amount) if counts[i] < reach]
        mass, left = sum([weights[i] for i in movable]), spare
        for i in movable:
            addition = min(reach - counts[i], max(1, left * weights[i] // mass), spare)
            counts[i] = counts[i] + addition
            spare = spare - addition
    return np.array(counts)


def noise(rng, extent, width, most, shards=(), kind=jnp.bfloat16):
    result = width * jax.random.normal(rng, extent, jnp.float32)
    if shards:
        result = result * level_of(rng, extent, shards, -0.22, 0.18)
    return jnp.clip(result, -most, most).astype(kind)


def setup_inputs(seed: int = 0) -> dict:
    key_list = jax.random.split(jax.random.key(seed), 10)
    section_acts = noise(key_list[0], (SECTIONS, TOKENS, D), 1.0, 6.0, ((0, 16), (1, 32)))
    section_grads = noise(key_list[1], (SECTIONS, TOKENS, D), 1.0, 6.0, ((0, 16), (1, 32)))
    routes_fwd_keys = jax.random.split(jax.random.fold_in(key_list[2], 1), SECTIONS * TOKENS // TOK_DEV)
    routes_fwd_turns = jax.random.permutation(jax.random.fold_in(key_list[2], 3), SECTIONS * TOKENS // TOK_DEV)
    routes_fwd = jax.vmap(lambda own, number: assign_block(jax.random.fold_in(key_list[2], 2), own, number, TOK_DEV, EXPERTS, TOP, CAP, 2))(routes_fwd_keys, routes_fwd_turns).reshape((SECTIONS, TOKENS, TOP))
    gate_fwd = set_ends(jax.random.randint(key_list[3], (SECTIONS, TOKENS, TOP), 32, 256), jax.random.fold_in(key_list[3], 1), 32, 255).astype(jnp.int32)
    routes_bwd_keys = jax.random.split(jax.random.fold_in(key_list[4], 1), SECTIONS * TOKENS // TOK_DEV)
    routes_bwd_turns = jax.random.permutation(jax.random.fold_in(key_list[4], 3), SECTIONS * TOKENS // TOK_DEV)
    routes_bwd = jax.vmap(lambda own, number: assign_block(jax.random.fold_in(key_list[4], 2), own, number, TOK_DEV, EXPERTS, TOP, CAP, 2))(routes_bwd_keys, routes_bwd_turns).reshape((SECTIONS, TOKENS, TOP))
    gate_bwd = set_ends(jax.random.randint(key_list[5], (SECTIONS, TOKENS, TOP), 32, 256), jax.random.fold_in(key_list[5], 1), 32, 255).astype(jnp.int32)
    saved_pre = noise(key_list[6], (SECTIONS, BLOCKS, BLOCKS, CAP, 2 * HID_DEV), 1.0, 6.0, ((0, 16), (1, 32)))
    w_gate_up = noise(key_list[7], (SECTIONS, BLOCKS, D, 2 * HID_DEV), D ** -0.5, 0.125, ((0, 16), (1, 32)))
    w_down = noise(key_list[8], (SECTIONS, BLOCKS, HID_DEV, D), H ** -0.5, 0.21875, ((0, 16), (1, 32)))
    return dict(section_acts=section_acts, section_grads=section_grads, routes_fwd=routes_fwd, gate_fwd=gate_fwd, routes_bwd=routes_bwd, gate_bwd=gate_bwd, saved_pre=saved_pre, w_gate_up=w_gate_up, w_down=w_down)


def slot_numbers(routes):
    assigned = routes.reshape(BLOCKS, TOK_DEV * TOP)
    onehot = (assigned[..., None] == jnp.arange(EXPERTS, dtype=jnp.int32)).astype(jnp.int32)
    earlier = jnp.cumsum(onehot, axis=1) - onehot
    return jnp.sum(earlier * onehot, axis=-1).reshape(TOKENS, TOP).astype(jnp.int32)


def slot_rows(routes):
    source = (jnp.arange(TOKENS, dtype=jnp.int32) // TOK_DEV)[:, None]
    return (routes * (BLOCKS * CAP) + source * CAP + slot_numbers(routes)).astype(jnp.int32)


def to_slots(values, routes):
    flat_rows = slot_rows(routes).reshape(TOKENS * TOP)
    repeated = jnp.repeat(values, TOP, axis=0)
    buffer = jnp.zeros((EXPERTS * BLOCKS * CAP, D), values.dtype)
    return buffer.at[flat_rows].set(repeated).reshape(EXPERTS, BLOCKS * CAP, D)


def expert_pass(operands):
    rows_in, rows_grad, inner_w, outer_w, saved_acts = operands
    fwd_total = jnp.zeros(rows_in.shape, jnp.float32)
    back_total = jnp.zeros(rows_in.shape, jnp.float32)
    for member in range(GROUP):
        projected = jnp.dot(rows_in, inner_w[member], preferred_element_type=jnp.float32)
        hidden_act = (jax.nn.silu(projected[:, :HID_DEV]) * projected[:, HID_DEV:]).astype(jnp.bfloat16)
        fwd_part = jnp.dot(hidden_act, outer_w[member], preferred_element_type=jnp.float32).astype(jnp.bfloat16)
        fwd_total = fwd_total + lax.optimization_barrier(fwd_part).astype(jnp.float32)
        gate_saved = saved_acts[member][:, :HID_DEV].astype(jnp.float32)
        up_saved = saved_acts[member][:, HID_DEV:].astype(jnp.float32)
        back_hidden = jnp.dot(rows_grad, outer_w[member].T, preferred_element_type=jnp.float32)
        sigmoid_gate = jax.nn.sigmoid(gate_saved)
        back_pre = jnp.concatenate(
            [back_hidden * up_saved * sigmoid_gate * (1.0 + gate_saved * (1.0 - sigmoid_gate)),
             back_hidden * gate_saved * sigmoid_gate], axis=-1).astype(jnp.bfloat16)
        back_part = jnp.dot(back_pre, inner_w[member].T, preferred_element_type=jnp.float32).astype(jnp.bfloat16)
        back_total = back_total + lax.optimization_barrier(back_part).astype(jnp.float32)
    return fwd_total.astype(jnp.bfloat16), back_total.astype(jnp.bfloat16)


def combine(residual_in, outputs, routes, gate_ints):
    picked = jnp.take(outputs.reshape(EXPERTS * BLOCKS * CAP, D), slot_rows(routes), axis=0).astype(jnp.float32)
    weights = gate_ints.astype(jnp.float32) / 128.0
    return (residual_in.astype(jnp.float32) + jnp.sum(picked * weights[..., None], axis=1)).astype(jnp.bfloat16)


def section_pass(operands):
    section_in, grad_in, routes_fwd, gate_fwd, routes_bwd, gate_bwd, saved_pre, w_gate_up, w_down = operands
    fwd_rows = to_slots(section_in, routes_fwd)
    back_rows = to_slots(grad_in, routes_bwd)
    fwd_out, back_out = lax.map(expert_pass, (
        fwd_rows, back_rows,
        w_gate_up.reshape(EXPERTS, GROUP, D, 2 * HID_DEV),
        w_down.reshape(EXPERTS, GROUP, HID_DEV, D),
        saved_pre.reshape(EXPERTS, GROUP, BLOCKS * CAP, 2 * HID_DEV)))
    moe_out = combine(section_in, fwd_out, routes_fwd, gate_fwd)
    input_grad = combine(grad_in, back_out, routes_bwd, gate_bwd)
    return moe_out, input_grad


def reference(section_acts, section_grads, routes_fwd, gate_fwd, routes_bwd, gate_bwd, saved_pre, w_gate_up, w_down):
    section_in = jnp.roll(section_acts, 1, axis=0)
    grad_in = jnp.roll(section_grads, -1, axis=0)
    moe_out, input_grad = lax.map(section_pass, (section_in, grad_in, routes_fwd, gate_fwd, routes_bwd, gate_bwd, saved_pre, w_gate_up, w_down))
    return moe_out, input_grad
```

```python
import functools

import jax
import jax.numpy as jnp
from jax import lax
from jax.experimental import pallas as pl
from jax.experimental.pallas import tpu as pltpu
from jax.sharding import PartitionSpec as P

MESH = pl.DeviceIdType.MESH
EXPERTS = 8
GROUP = 4
MAIN = 16
REST = 4
BF = jnp.bfloat16
F32 = jnp.float32


def dot(a, b, ca=1, cb=0):
    return lax.dot_general(a, b, (((ca,), (cb,)), ((), ())), preferred_element_type=F32)


def places(routes, gates, shift):
    tokens = routes.shape[0]
    rows_main, rows_mix = EXPERTS * MAIN, EXPERTS * 2 * REST
    lanes = lax.broadcasted_iota(jnp.int32, (tokens, 128), 1)
    names = [routes[:, k : k + 1] for k in range(2)]
    onehot = [(name == lanes).astype(F32) for name in names]
    row = lax.broadcasted_iota(jnp.int32, (tokens, tokens), 0)
    column = lax.broadcasted_iota(jnp.int32, (tokens, tokens), 1)
    before = dot((column < row).astype(BF), (onehot[0] + onehot[1]).astype(BF))
    main_at = lax.broadcasted_iota(jnp.int32, (tokens, rows_main), 1)
    mix_at = lax.broadcasted_iota(jnp.int32, (tokens, rows_mix), 1)
    sel = [jnp.zeros((tokens, rows_main), F32), jnp.zeros((tokens, rows_mix), F32)]
    comb = list(sel)
    for k in range(2):
        slot = jnp.sum(onehot[k] * before, axis=1, keepdims=True).astype(jnp.int32)
        gate = gates[:, k : k + 1].astype(F32) * (1.0 / 128.0)
        in_main = jnp.where(slot < MAIN, names[k] * MAIN + slot, -1)
        in_mix = jnp.where(slot < MAIN, -1, names[k] * (2 * REST) + shift + slot - MAIN)
        for i, hit in enumerate(((main_at == in_main), (mix_at == in_mix))):
            hit = hit.astype(F32)
            sel[i] = sel[i] + hit
            comb[i] = comb[i] + hit * gate
    return [s.T.astype(BF) for s in sel] + [c.astype(BF) for c in comb]


def kernel(
    n_pipe, n_expert,
    acts, grads, routes_f, gate_f, routes_b, gate_b, saved, gate_up, down,
    moe_out, input_grad,
    x_in, g_in, w_gu, w_d, sv,
    s_f, s_b, s_m, r_f, r_b, r_m,
    x_f, x_b, acc_f, acc_b,
    pipe_s, pipe_r, loc, plane_s, plane_r, z_s, z_r, z_l, q_s, q_r, q_l,
):
    width = acts.shape[1]
    hid = down.shape[0]
    pipe = lax.axis_index("pipe")
    me = lax.axis_index("expert")
    z = me // GROUP
    line = lax.rem(me, GROUP)
    nxt = {"pipe": lax.rem(pipe + 1, n_pipe)}
    prv = {"pipe": lax.rem(pipe + n_pipe - 1, n_pipe)}
    core = 1 - 2 * lax.rem(me, 2)
    side = 2 - 4 * lax.rem(me // 2, 2)
    mates = {1: me + core, 2: me + side, 3: me + core + side}

    def along(d):
        return lax.rem(z + d, EXPERTS)

    order = (4, 3, 5, 2, 6, 1, 7)
    partners = [nxt, prv] + [{"expert": mates[r]} for r in (1, 2, 3)]
    partners += [{"expert": along(d) * GROUP + line} for d in order]
    barrier = pltpu.get_barrier_semaphore()
    for partner in partners:
        pl.semaphore_signal(barrier, inc=1, device_id=partner, device_id_type=MESH)
    pl.semaphore_wait(barrier, len(partners))

    def remote(src, dst, ssem, rsem, to):
        return pltpu.make_async_remote_copy(
            src_ref=src, dst_ref=dst, send_sem=ssem, recv_sem=rsem, device_id=to, device_id_type=MESH
        )

    shift_f = remote(acts, x_in, pipe_s.at[0], pipe_r.at[0], nxt)
    shift_b = remote(grads, g_in, pipe_s.at[1], pipe_r.at[1], prv)
    shift_f.start()
    shift_b.start()

    half = gate_up.shape[0] // 2
    parts = [pl.ds(0, half), pl.ds(half, half)]

    def send_down(src, r, by):
        return remote(src, w_d.at[r], plane_s.at[r, 0], plane_r.at[r, 0], {"expert": mates[by]})

    def send_gu(src, r, by, i):
        return remote(src.at[parts[i]], w_gu.at[r, parts[i]], plane_s.at[r, 1 + i], plane_r.at[r, 1 + i], {"expert": mates[by]})

    def saved_to(r):
        to = mates[r]
        return remote(saved.at[lax.rem(to, GROUP)], sv.at[r], plane_s.at[r, 3], plane_r.at[r, 3], {"expert": to})

    own = [
        pltpu.make_async_copy(down, w_d.at[0], loc.at[0]),
        pltpu.make_async_copy(gate_up, w_gu.at[0], loc.at[1]),
        pltpu.make_async_copy(saved.at[line], sv.at[0], loc.at[2]),
    ]
    for copy in own:
        copy.start()
    across = {(2, 0): send_down(down, 2, 2), (2, 1): send_gu(gate_up, 2, 2, 0), (2, 2): send_gu(gate_up, 2, 2, 1)}
    beside = {(1, 0): send_down(down, 1, 1), (1, 1): send_gu(gate_up, 1, 1, 0), (1, 2): send_gu(gate_up, 1, 1, 1)}
    relayed = {(3, 0): send_down(w_d.at[2], 3, 1), (3, 1): send_gu(w_gu.at[2], 3, 1, 0), (3, 2): send_gu(w_gu.at[2], 3, 1, 1)}
    kept = {r: saved_to(r) for r in (1, 2, 3)}
    for copy in across.values():
        copy.start()
    for copy in beside.values():
        copy.start()
    for copy in kept.values():
        copy.start()

    sel_f, mix_f, comb_f, cmix_f = places(routes_f[...], gate_f[...], 0)
    sel_b, mix_b, comb_b, cmix_b = places(routes_b[...], gate_b[...], REST)

    step = 512
    chunks = width // step

    def columns(i):
        return pl.ds(pl.multiple_of(i * step, step), step)

    def travel(src, dst, sems, b, d):
        ssem, rsem = sems
        there = along(d)
        return remote(src.at[there], dst.at[z], ssem.at[b, d], rsem.at[b, d], {"expert": there * GROUP + line})

    def arrive(src, dst, sems, b, d):
        ssem, rsem = sems
        there = along(EXPERTS - d)
        return remote(src.at[there], dst.at[there], ssem.at[b, d], rsem.at[b, d], {"expert": there * GROUP + line})

    out_sems, back_sems = (z_s, z_r), (q_s, q_r)

    def start_all(src, dst, sems, local_sem, b):
        for d in order:
            travel(src, dst, sems, b, d).start()
        pltpu.make_async_copy(src.at[z], dst.at[z], local_sem.at[b]).start()

    def recv_all(src, dst, sems, local_sem, b):
        for d in order[::-1]:
            arrive(src, dst, sems, b, d).wait_recv()
        pltpu.make_async_copy(src.at[z], dst.at[z], local_sem.at[b]).wait()

    def sent_all(src, dst, sems, b):
        for d in order:
            travel(src, dst, sems, b, d).wait_send()

    shift_f.wait_recv()

    @pl.loop(0, chunks)
    def _(i):
        at = columns(i)
        s_f[:, :, at] = dot(sel_f, x_in[:, at]).astype(BF).reshape(EXPERTS, MAIN, step)

    start_all(s_f, r_f, out_sems, z_l, 0)
    shift_b.wait_recv()

    @pl.loop(0, chunks)
    def _(i):
        at = columns(i)
        s_b[:, :, at] = dot(sel_b, g_in[:, at]).astype(BF).reshape(EXPERTS, MAIN, step)
        both = dot(mix_f, x_in[:, at]) + dot(mix_b, g_in[:, at])
        s_m[:, :, at] = both.reshape(EXPERTS, 2 * REST, step).astype(BF)

    start_all(s_m, r_m, out_sems, z_l, 2)
    start_all(s_b, r_b, out_sems, z_l, 1)

    def relay(i):
        across[2, i].wait_recv()
        relayed[3, i].start()

    relay(0)
    for copy in own:
        copy.wait()
    for i in range(3):
        beside[1, i].wait_recv()

    def forward(r, first):
        proj = dot(x_f[...], w_gu[r])
        a, b = proj[:, :hid], proj[:, hid:]
        hidden = (a * (1.0 / (1.0 + jnp.exp(-a))) * b).astype(BF)

        @pl.loop(0, chunks)
        def _(i):
            at = columns(i)
            part = dot(hidden, w_d[r, :, at])
            acc_f[:, at] = part if first else acc_f[:, at] + part

    def backward(r, first):
        back_hidden = dot(x_b[...], w_d[r], 1, 1)
        pre = sv[r].astype(F32)
        g, u = pre[:, :hid], pre[:, hid:]
        sigma = 1.0 / (1.0 + jnp.exp(-g))
        back_pre = jnp.concatenate(
            [back_hidden * u * sigma * (1.0 + g * (1.0 - sigma)), back_hidden * g * sigma], axis=1
        ).astype(BF)

        @pl.loop(0, chunks)
        def _(i):
            at = columns(i)
            part = dot(back_pre, w_gu[r, at, :], 1, 1)
            acc_b[:, at] = part if first else acc_b[:, at] + part

    rows_main, rows_mix = EXPERTS * MAIN, EXPERTS * 2 * REST
    recv_all(s_f, r_f, out_sems, z_l, 0)
    recv_all(s_m, r_m, out_sems, z_l, 2)
    x_f[:rows_main, :] = r_f[...].reshape(rows_main, width)
    mixed = r_m[...].reshape(rows_mix, width)
    x_f[rows_main:, :] = mixed
    x_b[rows_main:, :] = mixed
    forward(0, True)
    forward(1, False)
    recv_all(s_b, r_b, out_sems, z_l, 1)
    x_b[:rows_main, :] = r_b[...].reshape(rows_main, width)
    kept[1].wait_recv()
    backward(0, True)
    backward(1, False)
    relay(1)
    relay(2)
    kept[2].wait_recv()
    forward(2, False)
    backward(2, False)
    for i in range(3):
        relayed[3, i].wait_recv()
    kept[3].wait_recv()
    for src, dst, b in ((s_f, r_f, 0), (s_m, r_m, 2), (s_b, r_b, 1)):
        sent_all(src, dst, out_sems, b)
    for d in order:
        pl.semaphore_signal(q_l.at[0], inc=1, device_id={"expert": along(d) * GROUP + line}, device_id_type=MESH)
    forward(3, False)

    @pl.loop(0, chunks)
    def _(i):
        at = columns(i)
        r_f[:, :, at] = acc_f[:rows_main, at].astype(BF).reshape(EXPERTS, MAIN, step)

    pl.semaphore_wait(q_l.at[0], len(order))
    start_all(r_f, s_f, back_sems, z_l, 0)
    backward(3, False)

    @pl.loop(0, chunks)
    def _(i):
        at = columns(i)
        r_b[:, :, at] = acc_b[:rows_main, at].astype(BF).reshape(EXPERTS, MAIN, step)
        row = lax.broadcasted_iota(jnp.int32, (rows_mix, step), 0)
        both = jnp.where(lax.rem(row, 2 * REST) < REST, acc_f[rows_main:, at], acc_b[rows_main:, at])
        r_m[:, :, at] = both.reshape(EXPERTS, 2 * REST, step).astype(BF)

    start_all(r_m, s_m, back_sems, z_l, 2)
    start_all(r_b, s_b, back_sems, z_l, 1)
    recv_all(r_f, s_f, back_sems, z_l, 0)
    recv_all(r_m, s_m, back_sems, z_l, 2)

    @pl.loop(0, chunks)
    def _(i):
        at = columns(i)
        main = s_f[:, :, at].reshape(rows_main, step)
        mix = s_m[:, :, at].reshape(rows_mix, step)
        moe_out[:, at] = (x_in[:, at].astype(F32) + dot(comb_f, main) + dot(cmix_f, mix)).astype(BF)

    recv_all(r_b, s_b, back_sems, z_l, 1)

    @pl.loop(0, chunks)
    def _(i):
        at = columns(i)
        main = s_b[:, :, at].reshape(rows_main, step)
        mix = s_m[:, :, at].reshape(rows_mix, step)
        input_grad[:, at] = (g_in[:, at].astype(F32) + dot(comb_b, main) + dot(cmix_b, mix)).astype(BF)

    for src, dst, b in ((r_f, s_f, 0), (r_m, s_m, 2), (r_b, s_b, 1)):
        sent_all(src, dst, back_sems, b)
    shift_f.wait_send()
    shift_b.wait_send()
    for copies in (across, beside, relayed, kept):
        for copy in copies.values():
            copy.wait_send()


def on_device(n_pipe, n_expert, acts, grads, routes_f, gate_f, routes_b, gate_b, saved, gate_up, down):
    tokens, width = acts.shape[1:]
    hid = down.shape[2]
    wide = gate_up.shape[3]
    rows_main, rows_mix = EXPERTS * MAIN, EXPERTS * 2 * REST
    rows = rows_main + rows_mix
    by_line = saved[0, 0].reshape(EXPERTS, GROUP, MAIN + REST, wide).transpose(1, 0, 2, 3)
    main = by_line[:, :, :MAIN].reshape(GROUP, rows_main, wide)
    mix = jnp.pad(by_line[:, :, MAIN:], ((0, 0), (0, 0), (REST, 0), (0, 0))).reshape(GROUP, rows_mix, wide)
    by_line = jnp.concatenate([main, mix], axis=1)

    vmem = pl.BlockSpec(memory_space=pltpu.VMEM)
    hbm = pl.BlockSpec(memory_space=pl.ANY)
    block = pltpu.VMEM((EXPERTS, MAIN, width), BF)
    mixed = pltpu.VMEM((EXPERTS, 2 * REST, width), BF)
    sems = pltpu.SemaphoreType.DMA
    out = jax.ShapeDtypeStruct((tokens, width), BF)
    moe_out, input_grad = pl.pallas_call(
        functools.partial(kernel, n_pipe, n_expert),
        out_shape=(out, out),
        in_specs=[hbm, hbm, vmem, vmem, vmem, vmem, hbm, hbm, hbm],
        out_specs=(vmem, vmem),
        scratch_shapes=[
            pltpu.VMEM((tokens, width), BF),
            pltpu.VMEM((tokens, width), BF),
            pltpu.VMEM((GROUP, width, wide), BF),
            pltpu.VMEM((GROUP, hid, width), BF),
            pltpu.VMEM((GROUP, rows, wide), BF),
            block, block, mixed, block, block, mixed,
            pltpu.VMEM((rows, width), BF),
            pltpu.VMEM((rows, width), BF),
            pltpu.VMEM((rows, width), F32),
            pltpu.VMEM((rows, width), F32),
            sems((2,)), sems((2,)), sems((3,)),
            sems((GROUP, 4)), sems((GROUP, 4)),
            sems((3, EXPERTS)), sems((3, EXPERTS)), sems((3,)),
            sems((3, EXPERTS)), sems((3, EXPERTS)),
            pltpu.SemaphoreType.REGULAR((1,)),
        ],
        compiler_params=pltpu.CompilerParams(
            collective_id=0, has_side_effects=True, vmem_limit_bytes=60 * 1024 * 1024
        ),
    )(acts[0], grads[0], routes_f[0], gate_f[0], routes_b[0], gate_b[0], by_line, gate_up[0, 0], down[0, 0])
    return moe_out[None], input_grad[None]


def solution(mesh):
    three = P("pipe", "expert", None)
    four = P("pipe", "expert", None, None)
    return jax.shard_map(
        functools.partial(on_device, mesh.shape["pipe"], mesh.shape["expert"]),
        mesh=mesh,
        in_specs=(three,) * 6 + (P("pipe", "expert", None, None, None), four, four),
        out_specs=(three, three),
        check_vma=False,
    )
```

```python
import functools

import jax
import jax.numpy as jnp
from jax import lax
from jax.experimental import pallas as pl
from jax.experimental.pallas import tpu as pltpu
from jax.sharding import PartitionSpec as P

MESH = pl.DeviceIdType.MESH
EXPERTS = 8
GROUP = 4
MAIN = 16
REST = 4
BF = jnp.bfloat16
F32 = jnp.float32
ROWS_MAIN = EXPERTS * MAIN
ROWS_MIX = EXPERTS * 2 * REST
ROWS = ROWS_MAIN + ROWS_MIX
CHUNKS = 4


def dot(a, b, ca=1, cb=0):
    return lax.dot_general(a, b, (((ca,), (cb,)), ((), ())), preferred_element_type=F32)


def places(routes, gates, shift):
    tokens = routes.shape[1]
    names = [routes[k : k + 1, :] for k in range(2)]
    experts = lax.broadcasted_iota(jnp.int32, (EXPERTS, tokens), 0)
    onehot = [(name == experts).astype(F32) for name in names]
    row = lax.broadcasted_iota(jnp.int32, (tokens, tokens), 0)
    column = lax.broadcasted_iota(jnp.int32, (tokens, tokens), 1)
    before = dot((onehot[0] + onehot[1]).astype(BF), (row < column).astype(BF))
    sel = [jnp.zeros((rows, tokens), F32) for rows in (ROWS_MAIN, ROWS_MIX)]
    at = [lax.broadcasted_iota(jnp.int32, s.shape, 0) for s in sel]
    comb = list(sel)
    for k in range(2):
        slot = jnp.sum(onehot[k] * before, axis=0, keepdims=True).astype(jnp.int32)
        gate = gates[k : k + 1, :].astype(F32) * (1.0 / 128.0)
        in_main = jnp.where(slot < MAIN, names[k] * MAIN + slot, -1)
        in_mix = jnp.where(slot < MAIN, -1, names[k] * (2 * REST) + shift + slot - MAIN)
        for i, place in enumerate((in_main, in_mix)):
            hit = (at[i] == place).astype(F32)
            sel[i] = sel[i] + hit
            comb[i] = comb[i] + hit * gate
    return [s.astype(BF) for s in sel] + [c.T.astype(BF) for c in comb]


def kernel(
    n_pipe,
    acts, grads, routes_f, gate_f, routes_b, gate_b, saved, gate_up, down,
    moe_out, input_grad,
    x_in, g_in, w_gu, w_d, raw, sv_out, sv,
    s_f, s_b, s_m, r_f, r_b, r_m,
    y_f, y_b, y_m, h_f, h_b, h_m,
    x_f, x_b, pre_b, proj_f, hid_f,
    pipe_s, pipe_r, loc, plane_s, plane_r, z_s, z_r, z_l, q_s, q_r, q_l,
):
    width = acts.shape[1]
    hid = down.shape[0]
    step = width // CHUNKS
    pipe = lax.axis_index("pipe")
    me = lax.axis_index("expert")
    z = me // GROUP
    line = lax.rem(me, GROUP)
    nxt = {"pipe": lax.rem(pipe + 1, n_pipe)}
    prv = {"pipe": lax.rem(pipe + n_pipe - 1, n_pipe)}
    core = 1 - 2 * lax.rem(me, 2)
    side = 2 - 4 * lax.rem(me // 2, 2)
    mates = {1: me + core, 2: me + side, 3: me + core + side}

    def along(d):
        return lax.rem(z + d, EXPERTS)

    order = (4, 3, 5, 2, 6, 1, 7)
    load_raw = pltpu.make_async_copy(saved, raw, loc.at[3])
    load_raw.start()
    own = [
        pltpu.make_async_copy(down, w_d.at[0], loc.at[0]),
        pltpu.make_async_copy(gate_up, w_gu.at[0], loc.at[1]),
    ]
    for copy in own:
        copy.start()
    partners = [nxt, prv] + [{"expert": mates[r]} for r in (1, 2, 3)]
    partners += [{"expert": along(d) * GROUP + line} for d in order]
    barrier = pltpu.get_barrier_semaphore()
    for partner in partners:
        pl.semaphore_signal(barrier, inc=1, device_id=partner, device_id_type=MESH)
    pl.semaphore_wait(barrier, len(partners))

    def remote(src, dst, ssem, rsem, to):
        return pltpu.make_async_remote_copy(
            src_ref=src, dst_ref=dst, send_sem=ssem, recv_sem=rsem, device_id=to, device_id_type=MESH
        )

    shift_f = remote(acts, x_in, pipe_s.at[0], pipe_r.at[0], nxt)
    shift_b = remote(grads, g_in, pipe_s.at[1], pipe_r.at[1], prv)
    shift_b.start()
    shift_f.start()

    parts = [pl.ds(i * step, step) for i in range(CHUNKS)]

    def send_down(src, r, by):
        return remote(src, w_d.at[r], plane_s.at[r, 0], plane_r.at[r, 0], {"expert": mates[by]})

    def send_gu(src, r, by, i):
        at = 2 + i
        return remote(src.at[parts[i]], w_gu.at[r, parts[i]], plane_s.at[r, at], plane_r.at[r, at], {"expert": mates[by]})

    def saved_to(r):
        to = mates[r]
        return remote(sv_out.at[lax.rem(to, GROUP)], sv.at[r], plane_s.at[r, 1], plane_r.at[r, 1], {"expert": to})

    downs = {1: send_down(down, 1, 1), 2: send_down(down, 2, 2), 3: send_down(w_d.at[2], 3, 1)}
    gus = {1: [send_gu(gate_up, 1, 1, i) for i in range(CHUNKS)]}
    gus[2] = [send_gu(gate_up, 2, 2, i) for i in range(CHUNKS)]
    gus[3] = [send_gu(w_gu.at[2], 3, 1, i) for i in range(CHUNKS)]
    kept = {r: saved_to(r) for r in (1, 2, 3)}
    downs[2].start()
    downs[1].start()

    load_raw.wait()
    flat = raw[...].reshape(raw.shape[0] * raw.shape[1], raw.shape[2])
    row = lax.broadcasted_iota(jnp.int32, (ROWS, flat.shape[0]), 0)
    column = lax.broadcasted_iota(jnp.int32, (ROWS, flat.shape[0]), 1)
    late = row - ROWS_MAIN
    slot = jnp.where(late < 0, row & (MAIN - 1), MAIN - REST + (late & (2 * REST - 1)))
    plane = jnp.where(late < 0, row >> 4, late >> 3)
    known = (late < 0) | (slot >= MAIN)
    base = jnp.where(known, slot * raw.shape[1] + plane * GROUP, -GROUP)
    for number in range(GROUP):
        pick = (column == base + number).astype(BF)
        sv_out[number] = dot(pick, flat).astype(BF)
    keep_own = pltpu.make_async_copy(sv_out.at[line], sv.at[0], loc.at[2])
    keep_own.start()
    for r in (2, 3, 1):
        kept[r].start()
    for i in range(CHUNKS):
        gus[2][i].start()
        gus[1][i].start()

    sel_f, mix_f, comb_f, cmix_f = places(routes_f[...], gate_f[...], 0)
    sel_b, mix_b, comb_b, cmix_b = places(routes_b[...], gate_b[...], REST)

    def columns(i):
        return pl.ds(pl.multiple_of(i * step, step), step)

    everything = pl.ds(0, width)

    def travel(src, dst, sems, b, d, at):
        ssem, rsem = sems
        there = along(d)
        return remote(
            src.at[there, :, at], dst.at[z, :, at], ssem.at[b, d], rsem.at[b, d], {"expert": there * GROUP + line}
        )

    def arrive(src, dst, sems, b, d, at):
        ssem, rsem = sems
        there = along(EXPERTS - d)
        return remote(
            src.at[there, :, at], dst.at[there, :, at], ssem.at[b, d], rsem.at[b, d], {"expert": there * GROUP + line}
        )

    def start_all(src, dst, sems, local_sem, b, at):
        for d in order:
            travel(src, dst, sems, b, d, at).start()
        pltpu.make_async_copy(src.at[z, :, at], dst.at[z, :, at], local_sem.at[b]).start()

    def recv_all(src, dst, sems, local_sem, b, at):
        for d in order[::-1]:
            arrive(src, dst, sems, b, d, at).wait_recv()
        pltpu.make_async_copy(src.at[z, :, at], dst.at[z, :, at], local_sem.at[b]).wait()

    def sent_all(src, dst, sems, b, at):
        for d in order:
            travel(src, dst, sems, b, d, at).wait_send()

    out_sems, back_sems = (z_s, z_r), (q_s, q_r)

    shift_b.wait_recv()

    @pl.loop(0, CHUNKS)
    def _(i):
        at = columns(i)
        s_b[:, :, at] = dot(sel_b, g_in[:, at]).astype(BF).reshape(EXPERTS, MAIN, step)

    start_all(s_b, r_b, out_sems, z_l, 1, everything)
    shift_f.wait_recv()

    @pl.loop(0, CHUNKS)
    def _(i):
        at = columns(i)
        both = dot(mix_f, x_in[:, at]) + dot(mix_b, g_in[:, at])
        s_m[:, :, at] = both.reshape(EXPERTS, 2 * REST, step).astype(BF)

    start_all(s_m, r_m, out_sems, z_l, 2, everything)

    @pl.loop(0, CHUNKS)
    def _(i):
        at = columns(i)
        s_f[:, :, at] = dot(sel_f, x_in[:, at]).astype(BF).reshape(EXPERTS, MAIN, step)

    start_all(s_f, r_f, out_sems, z_l, 0, everything)

    for copy in own:
        copy.wait()
    keep_own.wait()
    downs[2].wait_recv()
    downs[3].start()
    recv_all(s_b, r_b, out_sems, z_l, 1, everything)
    x_b[:ROWS_MAIN, :] = r_b[...].reshape(ROWS_MAIN, width)
    recv_all(s_m, r_m, out_sems, z_l, 2, everything)
    mixed = r_m[...].reshape(ROWS_MIX, width)
    x_f[ROWS_MAIN:, :] = mixed
    x_b[ROWS_MAIN:, :] = mixed
    for r in range(GROUP):
        if r in (1, 3):
            downs[r].wait_recv()
        if r:
            kept[r].wait_recv()
        back_hidden = dot(x_b[...], w_d[r], 1, 1)
        pre = sv[r].astype(F32)
        g, u = pre[:, :hid], pre[:, hid:]
        sigma = 1.0 / (1.0 + jnp.exp(-g))
        pre_b[r] = jnp.concatenate(
            [back_hidden * u * sigma * (1.0 + g * (1.0 - sigma)), back_hidden * g * sigma], axis=1
        ).astype(BF)

    def backward(i):
        at = parts[i]
        gus[2][i].wait_recv()
        gus[3][i].start()
        gus[1][i].wait_recv()
        total = dot(pre_b[0], w_gu[0, at, :], 1, 1)
        total = total + dot(pre_b[1], w_gu[1, at, :], 1, 1)
        total = total + dot(pre_b[2], w_gu[2, at, :], 1, 1)
        gus[3][i].wait_recv()
        total = total + dot(pre_b[3], w_gu[3, at, :], 1, 1)
        y_b[:, :, at] = total[:ROWS_MAIN].astype(BF).reshape(EXPERTS, MAIN, step)
        y_m[:, :, at] = total[ROWS_MAIN:].astype(BF).reshape(EXPERTS, 2 * REST, step)
        start_all(y_b, h_b, back_sems, q_l, 2 * CHUNKS + i, at)

    def project(i):
        at = parts[i]
        for r in range(GROUP):
            part = dot(x_f[:, at], w_gu[r, at, :])
            proj_f[r] = part if i == 0 else proj_f[r] + part

    for i in range(CHUNKS):
        backward(i)
        if i == 1:
            recv_all(s_f, r_f, out_sems, z_l, 0, everything)
            x_f[:ROWS_MAIN, :] = r_f[...].reshape(ROWS_MAIN, width)
            project(0)
        if i:
            project(i)
    for r in range(GROUP):
        a, b = proj_f[r, :, :hid], proj_f[r, :, hid:]
        hid_f[r] = (a * (1.0 / (1.0 + jnp.exp(-a))) * b).astype(BF)
    from_forward = (lax.broadcasted_iota(jnp.int32, (ROWS_MIX, step), 0) & (2 * REST - 1)) < REST
    for i in range(CHUNKS):
        at = parts[i]
        total = dot(hid_f[0], w_d[0, :, at])
        for r in range(1, GROUP):
            total = total + dot(hid_f[r], w_d[r, :, at])
        y_f[:, :, at] = total[:ROWS_MAIN].astype(BF).reshape(EXPERTS, MAIN, step)
        other = y_m[:, :, at].reshape(ROWS_MIX, step).astype(F32)
        y_m[:, :, at] = (
            jnp.where(from_forward, total[ROWS_MAIN:], other).reshape(EXPERTS, 2 * REST, step).astype(BF)
        )
        start_all(y_f, h_f, back_sems, q_l, i, at)
        start_all(y_m, h_m, back_sems, q_l, CHUNKS + i, at)

    for i in range(CHUNKS):
        recv_all(y_b, h_b, back_sems, q_l, 2 * CHUNKS + i, parts[i])
    for i in range(CHUNKS):
        at = parts[i]
        recv_all(y_f, h_f, back_sems, q_l, i, at)
        recv_all(y_m, h_m, back_sems, q_l, CHUNKS + i, at)
        mix = h_m[:, :, at].reshape(ROWS_MIX, step)
        main = h_f[:, :, at].reshape(ROWS_MAIN, step)
        moe_out[:, at] = (x_in[:, at].astype(F32) + dot(comb_f, main) + dot(cmix_f, mix)).astype(BF)
        main = h_b[:, :, at].reshape(ROWS_MAIN, step)
        input_grad[:, at] = (g_in[:, at].astype(F32) + dot(comb_b, main) + dot(cmix_b, mix)).astype(BF)

    for src, dst, b in ((s_f, r_f, 0), (s_b, r_b, 1), (s_m, r_m, 2)):
        sent_all(src, dst, out_sems, b, everything)
    for i in range(CHUNKS):
        for src, dst, b in ((y_f, h_f, 0), (y_m, h_m, 1), (y_b, h_b, 2)):
            sent_all(src, dst, back_sems, b * CHUNKS + i, parts[i])
    shift_f.wait_send()
    shift_b.wait_send()
    for r in (1, 2, 3):
        downs[r].wait_send()
        kept[r].wait_send()
        for copy in gus[r]:
            copy.wait_send()


def write_out(a, b, out_a, out_b, sem):
    copies = [pltpu.make_async_copy(a, out_a, sem.at[0]), pltpu.make_async_copy(b, out_b, sem.at[1])]
    for copy in copies:
        copy.start()
    for copy in copies:
        copy.wait()


def on_device(n_pipe, acts, grads, routes_f, gate_f, routes_b, gate_b, saved, gate_up, down):
    tokens, width = acts.shape[1:]
    hid = down.shape[2]
    wide = gate_up.shape[3]
    vmem = pl.BlockSpec(memory_space=pltpu.VMEM)
    hbm = pl.BlockSpec(memory_space=pl.ANY)
    block = pltpu.VMEM((EXPERTS, MAIN, width), BF)
    mixed = pltpu.VMEM((EXPERTS, 2 * REST, width), BF)
    sems = pltpu.SemaphoreType.DMA
    out = jax.ShapeDtypeStruct((tokens, width), BF)
    by_slot = saved[0, 0].transpose(1, 0, 2)
    results = pl.pallas_call(
        functools.partial(kernel, n_pipe),
        out_shape=(out, out),
        in_specs=[hbm, hbm, vmem, vmem, vmem, vmem, hbm, hbm, hbm],
        out_specs=(vmem, vmem),
        scratch_shapes=[
            pltpu.VMEM((tokens, width), BF),
            pltpu.VMEM((tokens, width), BF),
            pltpu.VMEM((GROUP, width, wide), BF),
            pltpu.VMEM((GROUP, hid, width), BF),
            pltpu.VMEM(by_slot.shape, BF),
            pltpu.VMEM((GROUP, ROWS, wide), BF),
            pltpu.VMEM((GROUP, ROWS, wide), BF),
            block, block, mixed, block, block, mixed,
            block, block, mixed, block, block, mixed,
            pltpu.VMEM((ROWS, width), BF),
            pltpu.VMEM((ROWS, width), BF),
            pltpu.VMEM((GROUP, ROWS, wide), BF),
            pltpu.VMEM((GROUP, ROWS, wide), F32),
            pltpu.VMEM((GROUP, ROWS, hid), BF),
            sems((2,)), sems((2,)), sems((4,)),
            sems((GROUP, 2 + CHUNKS)), sems((GROUP, 2 + CHUNKS)),
            sems((3, EXPERTS)), sems((3, EXPERTS)), sems((3,)),
            sems((3 * CHUNKS, EXPERTS)), sems((3 * CHUNKS, EXPERTS)), sems((3 * CHUNKS,)),
        ],
        compiler_params=pltpu.CompilerParams(
            collective_id=0, has_side_effects=True, vmem_limit_bytes=60 * 1024 * 1024
        ),
    )(
        acts[0], grads[0], routes_f[0].T, gate_f[0].T, routes_b[0].T, gate_b[0].T,
        by_slot, gate_up[0, 0], down[0, 0],
    )
    moe_out, input_grad = pl.pallas_call(
        write_out,
        out_shape=(out, out),
        in_specs=[vmem, vmem],
        out_specs=(hbm, hbm),
        scratch_shapes=[sems((2,))],
    )(*results)
    return moe_out[None], input_grad[None]


def solution(mesh):
    three = P("pipe", "expert", None)
    four = P("pipe", "expert", None, None)
    return jax.shard_map(
        functools.partial(on_device, mesh.shape["pipe"]),
        mesh=mesh,
        in_specs=(three,) * 6 + (P("pipe", "expert", None, None, None), four, four),
        out_specs=(three, three),
        check_vma=False,
    )
```

```python
import functools

import jax
import jax.numpy as jnp
from jax import lax
from jax.experimental import pallas as pl
from jax.experimental.pallas import tpu as pltpu
from jax.sharding import PartitionSpec as P

MESH = pl.DeviceIdType.MESH
EXPERTS = 8
GROUP = 4
MAIN = 16
REST = 4
BF = jnp.bfloat16
F32 = jnp.float32
ROWS_MAIN = EXPERTS * MAIN
ROWS_MIX = EXPERTS * 2 * REST
ROWS = ROWS_MAIN + ROWS_MIX
PARTS = (768, 768, 640, 384)
CHUNKS = len(PARTS)
STEPS = 4


def dot(a, b, ca=1, cb=0):
    return lax.dot_general(a, b, (((ca,), (cb,)), ((), ())), preferred_element_type=F32)


def places(routes, gates, shift):
    tokens = routes.shape[1]
    names = [routes[k : k + 1, :] for k in range(2)]
    experts = lax.broadcasted_iota(jnp.int32, (EXPERTS, tokens), 0)
    onehot = [(name == experts).astype(F32) for name in names]
    row = lax.broadcasted_iota(jnp.int32, (tokens, tokens), 0)
    column = lax.broadcasted_iota(jnp.int32, (tokens, tokens), 1)
    before = dot((onehot[0] + onehot[1]).astype(BF), (row < column).astype(BF))
    sel = [jnp.zeros((rows, tokens), F32) for rows in (ROWS_MAIN, ROWS_MIX)]
    at = [lax.broadcasted_iota(jnp.int32, s.shape, 0) for s in sel]
    comb = list(sel)
    for k in range(2):
        slot = jnp.sum(onehot[k] * before, axis=0, keepdims=True).astype(jnp.int32)
        gate = gates[k : k + 1, :].astype(F32) * (1.0 / 128.0)
        in_main = jnp.where(slot < MAIN, names[k] * MAIN + slot, -1)
        in_mix = jnp.where(slot < MAIN, -1, names[k] * (2 * REST) + shift + slot - MAIN)
        for i, place in enumerate((in_main, in_mix)):
            hit = (at[i] == place).astype(F32)
            sel[i] = sel[i] + hit
            comb[i] = comb[i] + hit * gate
    return [s.astype(BF) for s in sel] + [c.T.astype(BF) for c in comb]


def kernel(
    n_pipe,
    acts, grads, routes_f, gate_f, routes_b, gate_b, saved, gate_up, down,
    moe_out, input_grad,
    x_in, g_in, w_gu, w_d, raw, sv_out, sv,
    s_f, s_b, s_m, r_f, r_b, r_m,
    y_f, y_b, y_m, h_f, h_b, h_m,
    x_f, x_b, pre_b, proj_f, hid_f,
    meta, o_f, o_b, fin_f, fin_b,
    pipe_s, pipe_r, loc, plane_s, plane_r, z_s, z_r, z_l, q_s, q_r, q_l, fin_s, fin_r, meta_s, meta_r,
):
    width = acts.shape[1]
    hid = down.shape[0]
    step = width // STEPS
    pipe = lax.axis_index("pipe")
    me = lax.axis_index("expert")
    z = me // GROUP
    line = lax.rem(me, GROUP)
    core = 1 - 2 * lax.rem(me, 2)
    side = 2 - 4 * lax.rem(me // 2, 2)
    mates = {0: me, 1: me + core, 2: me + side, 3: me + core + side}
    nxt = {"pipe": lax.rem(pipe + 1, n_pipe), "expert": mates[2]}
    prv = {"pipe": lax.rem(pipe + n_pipe - 1, n_pipe), "expert": mates[2]}
    pair = {"expert": mates[2]}

    def along(d):
        return lax.rem(z + d, EXPERTS)

    order = (4, 3, 5, 2, 6, 1, 7)
    load_raw = pltpu.make_async_copy(saved, raw, loc.at[3])
    load_raw.start()
    own = [
        pltpu.make_async_copy(down, w_d.at[0], loc.at[0]),
        pltpu.make_async_copy(gate_up, w_gu.at[0], loc.at[1]),
    ]
    for copy in own:
        copy.start()
    partners = [nxt, prv] + [{"expert": mates[r]} for r in (1, 2, 3)]
    partners += [{"expert": along(d) * GROUP + line} for d in order]
    barrier = pltpu.get_barrier_semaphore()
    for partner in partners:
        pl.semaphore_signal(barrier, inc=1, device_id=partner, device_id_type=MESH)
    pl.semaphore_wait(barrier, len(partners))

    def remote(src, dst, ssem, rsem, to):
        return pltpu.make_async_remote_copy(
            src_ref=src, dst_ref=dst, send_sem=ssem, recv_sem=rsem, device_id=to, device_id_type=MESH
        )

    shift_f = remote(acts, x_in, pipe_s.at[0], pipe_r.at[0], nxt)
    shift_b = remote(grads, g_in, pipe_s.at[1], pipe_r.at[1], prv)
    tables = [
        remote(table, meta.at[k], meta_s.at[k], meta_r.at[k], pair)
        for k, table in enumerate((routes_f, gate_f, routes_b, gate_b))
    ]
    for copy in tables:
        copy.start()
    shift_b.start()
    shift_f.start()

    parts = [pl.ds(sum(PARTS[:i]), PARTS[i]) for i in range(CHUNKS)]

    def send_down(src, r, by):
        return remote(src, w_d.at[r], plane_s.at[r, 0], plane_r.at[r, 0], {"expert": mates[by]})

    def send_gu(src, r, by, i):
        at = 2 + i
        return remote(src.at[parts[i]], w_gu.at[r, parts[i]], plane_s.at[r, at], plane_r.at[r, at], {"expert": mates[by]})

    def saved_to(r):
        to = mates[r]
        return remote(sv_out.at[lax.rem(mates[r ^ 2], GROUP)], sv.at[r], plane_s.at[r, 1], plane_r.at[r, 1], {"expert": to})

    downs = {1: send_down(down, 1, 1), 2: send_down(down, 2, 2), 3: send_down(w_d.at[2], 3, 1)}
    gus = {1: [send_gu(gate_up, 1, 1, i) for i in range(CHUNKS)]}
    gus[2] = [send_gu(gate_up, 2, 2, i) for i in range(CHUNKS)]
    gus[3] = [send_gu(w_gu.at[2], 3, 1, i) for i in range(CHUNKS)]
    kept = {r: saved_to(r) for r in (1, 2, 3)}
    downs[2].start()
    downs[1].start()

    load_raw.wait()
    flat = raw[...].reshape(raw.shape[0] * raw.shape[1], raw.shape[2])
    row = lax.broadcasted_iota(jnp.int32, (ROWS, flat.shape[0]), 0)
    column = lax.broadcasted_iota(jnp.int32, (ROWS, flat.shape[0]), 1)
    late = row - ROWS_MAIN
    slot = jnp.where(late < 0, row & (MAIN - 1), MAIN - REST + (late & (2 * REST - 1)))
    plane = jnp.where(late < 0, row >> 4, late >> 3)
    known = (late < 0) | (slot >= MAIN)
    base = jnp.where(known, slot * raw.shape[1] + plane * GROUP, -GROUP)
    for number in range(GROUP):
        pick = (column == base + number).astype(BF)
        sv_out[number] = dot(pick, flat).astype(BF)
    keep_own = pltpu.make_async_copy(sv_out.at[lax.rem(mates[2], GROUP)], sv.at[0], loc.at[2])
    keep_own.start()
    for r in (2, 3, 1):
        kept[r].start()
    for i in range(CHUNKS):
        gus[2][i].start()
        gus[1][i].start()

    for copy in tables:
        copy.wait_recv()
    sel_f, mix_f, comb_f, cmix_f = places(meta[0], meta[1], 0)
    sel_b, mix_b, comb_b, cmix_b = places(meta[2], meta[3], REST)

    def columns(i):
        return pl.ds(pl.multiple_of(i * step, step), step)

    everything = pl.ds(0, width)

    def travel(src, dst, sems, b, d, at):
        ssem, rsem = sems
        there = along(d)
        return remote(
            src.at[there, :, at], dst.at[z, :, at], ssem.at[b, d], rsem.at[b, d], {"expert": there * GROUP + line}
        )

    def arrive(src, dst, sems, b, d, at):
        ssem, rsem = sems
        there = along(EXPERTS - d)
        return remote(
            src.at[there, :, at], dst.at[there, :, at], ssem.at[b, d], rsem.at[b, d], {"expert": there * GROUP + line}
        )

    def start_all(src, dst, sems, local_sem, b, at):
        for d in order:
            travel(src, dst, sems, b, d, at).start()
        pltpu.make_async_copy(src.at[z, :, at], dst.at[z, :, at], local_sem.at[b]).start()

    def recv_all(src, dst, sems, local_sem, b, at):
        for d in order[::-1]:
            arrive(src, dst, sems, b, d, at).wait_recv()
        pltpu.make_async_copy(src.at[z, :, at], dst.at[z, :, at], local_sem.at[b]).wait()

    def sent_all(src, dst, sems, b, at):
        for d in order:
            travel(src, dst, sems, b, d, at).wait_send()

    out_sems, back_sems = (z_s, z_r), (q_s, q_r)

    shift_b.wait_recv()

    @pl.loop(0, STEPS)
    def _(i):
        at = columns(i)
        s_b[:, :, at] = dot(sel_b, g_in[:, at]).astype(BF).reshape(EXPERTS, MAIN, step)

    start_all(s_b, r_b, out_sems, z_l, 1, everything)
    shift_f.wait_recv()

    @pl.loop(0, STEPS)
    def _(i):
        at = columns(i)
        both = dot(mix_f, x_in[:, at]) + dot(mix_b, g_in[:, at])
        s_m[:, :, at] = both.reshape(EXPERTS, 2 * REST, step).astype(BF)

    start_all(s_m, r_m, out_sems, z_l, 2, everything)

    @pl.loop(0, STEPS)
    def _(i):
        at = columns(i)
        s_f[:, :, at] = dot(sel_f, x_in[:, at]).astype(BF).reshape(EXPERTS, MAIN, step)

    start_all(s_f, r_f, out_sems, z_l, 0, everything)

    for copy in own:
        copy.wait()
    keep_own.wait()
    downs[2].wait_recv()
    downs[3].start()
    recv_all(s_b, r_b, out_sems, z_l, 1, everything)
    x_b[:ROWS_MAIN, :] = r_b[...].reshape(ROWS_MAIN, width)
    recv_all(s_m, r_m, out_sems, z_l, 2, everything)
    mixed = r_m[...].reshape(ROWS_MIX, width)
    x_f[ROWS_MAIN:, :] = mixed
    x_b[ROWS_MAIN:, :] = mixed
    for r in range(GROUP):
        if r in (1, 3):
            downs[r].wait_recv()
        if r:
            kept[r].wait_recv()
        back_hidden = dot(x_b[...], w_d[r], 1, 1)
        pre = sv[r].astype(F32)
        g, u = pre[:, :hid], pre[:, hid:]
        sigma = 1.0 / (1.0 + jnp.exp(-g))
        pre_b[r] = jnp.concatenate(
            [back_hidden * u * sigma * (1.0 + g * (1.0 - sigma)), back_hidden * g * sigma], axis=1
        ).astype(BF)

    def backward(i):
        at = parts[i]
        gus[2][i].wait_recv()
        gus[3][i].start()
        gus[1][i].wait_recv()
        total = dot(pre_b[0], w_gu[0, at, :], 1, 1)
        total = total + dot(pre_b[1], w_gu[1, at, :], 1, 1)
        total = total + dot(pre_b[2], w_gu[2, at, :], 1, 1)
        gus[3][i].wait_recv()
        total = total + dot(pre_b[3], w_gu[3, at, :], 1, 1)
        y_b[:, :, at] = total[:ROWS_MAIN].astype(BF).reshape(EXPERTS, MAIN, PARTS[i])
        y_m[:, :, at] = total[ROWS_MAIN:].astype(BF).reshape(EXPERTS, 2 * REST, PARTS[i])
        start_all(y_b, h_b, back_sems, q_l, 2 * CHUNKS + i, at)

    def project(i):
        at = parts[i]
        for r in range(GROUP):
            part = dot(x_f[:, at], w_gu[r, at, :])
            proj_f[r] = part if i == 0 else proj_f[r] + part

    for i in range(CHUNKS):
        backward(i)
        if i == 1:
            recv_all(s_f, r_f, out_sems, z_l, 0, everything)
            x_f[:ROWS_MAIN, :] = r_f[...].reshape(ROWS_MAIN, width)
            project(0)
        if i:
            project(i)
    for r in range(GROUP):
        a, b = proj_f[r, :, :hid], proj_f[r, :, hid:]
        hid_f[r] = (a * (1.0 / (1.0 + jnp.exp(-a))) * b).astype(BF)
    for i in range(CHUNKS):
        at = parts[i]
        shape = (ROWS_MIX, PARTS[i])
        total = dot(hid_f[0], w_d[0, :, at])
        for r in range(1, GROUP):
            total = total + dot(hid_f[r], w_d[r, :, at])
        y_f[:, :, at] = total[:ROWS_MAIN].astype(BF).reshape(EXPERTS, MAIN, PARTS[i])
        from_forward = (lax.broadcasted_iota(jnp.int32, shape, 0) & (2 * REST - 1)) < REST
        other = y_m[:, :, at].reshape(shape).astype(F32)
        both = jnp.where(from_forward, total[ROWS_MAIN:], other)
        y_m[:, :, at] = both.reshape(EXPERTS, 2 * REST, PARTS[i]).astype(BF)
        start_all(y_f, h_f, back_sems, q_l, i, at)
        start_all(y_m, h_m, back_sems, q_l, CHUNKS + i, at)

    def finished(i):
        at = parts[i]
        return [
            remote(o_f.at[:, at], fin_f.at[:, at], fin_s.at[0, i], fin_r.at[0, i], pair),
            remote(o_b.at[:, at], fin_b.at[:, at], fin_s.at[1, i], fin_r.at[1, i], pair),
        ]

    for i in range(CHUNKS):
        recv_all(y_b, h_b, back_sems, q_l, 2 * CHUNKS + i, parts[i])
    for i in range(CHUNKS):
        at = parts[i]
        recv_all(y_f, h_f, back_sems, q_l, i, at)
        recv_all(y_m, h_m, back_sems, q_l, CHUNKS + i, at)
        mix = h_m[:, :, at].reshape(ROWS_MIX, PARTS[i])
        main = h_f[:, :, at].reshape(ROWS_MAIN, PARTS[i])
        o_f[:, at] = (x_in[:, at].astype(F32) + dot(comb_f, main) + dot(cmix_f, mix)).astype(BF)
        main = h_b[:, :, at].reshape(ROWS_MAIN, PARTS[i])
        o_b[:, at] = (g_in[:, at].astype(F32) + dot(comb_b, main) + dot(cmix_b, mix)).astype(BF)
        for copy in finished(i):
            copy.start()
    for i in range(CHUNKS):
        at = parts[i]
        for copy in finished(i):
            copy.wait_recv()
        moe_out[:, at] = fin_f[:, at]
        input_grad[:, at] = fin_b[:, at]

    for copy in tables:
        copy.wait_send()
    for i in range(CHUNKS):
        for copy in finished(i):
            copy.wait_send()
    for src, dst, b in ((s_f, r_f, 0), (s_b, r_b, 1), (s_m, r_m, 2)):
        sent_all(src, dst, out_sems, b, everything)
    for i in range(CHUNKS):
        for src, dst, b in ((y_f, h_f, 0), (y_m, h_m, 1), (y_b, h_b, 2)):
            sent_all(src, dst, back_sems, b * CHUNKS + i, parts[i])
    shift_f.wait_send()
    shift_b.wait_send()
    for r in (1, 2, 3):
        downs[r].wait_send()
        kept[r].wait_send()
        for copy in gus[r]:
            copy.wait_send()


def write_out(a, b, out_a, out_b, sem):
    copies = [pltpu.make_async_copy(a, out_a, sem.at[0]), pltpu.make_async_copy(b, out_b, sem.at[1])]
    for copy in copies:
        copy.start()
    for copy in copies:
        copy.wait()


def on_device(n_pipe, acts, grads, routes_f, gate_f, routes_b, gate_b, saved, gate_up, down):
    tokens, width = acts.shape[1:]
    hid = down.shape[2]
    wide = gate_up.shape[3]
    vmem = pl.BlockSpec(memory_space=pltpu.VMEM)
    hbm = pl.BlockSpec(memory_space=pl.ANY)
    block = pltpu.VMEM((EXPERTS, MAIN, width), BF)
    mixed = pltpu.VMEM((EXPERTS, 2 * REST, width), BF)
    sems = pltpu.SemaphoreType.DMA
    out = jax.ShapeDtypeStruct((tokens, width), BF)
    by_slot = saved[0, 0].transpose(1, 0, 2)
    results = pl.pallas_call(
        functools.partial(kernel, n_pipe),
        out_shape=(out, out),
        in_specs=[hbm, hbm, vmem, vmem, vmem, vmem, hbm, hbm, hbm],
        out_specs=(vmem, vmem),
        scratch_shapes=[
            pltpu.VMEM((tokens, width), BF),
            pltpu.VMEM((tokens, width), BF),
            pltpu.VMEM((GROUP, width, wide), BF),
            pltpu.VMEM((GROUP, hid, width), BF),
            pltpu.VMEM(by_slot.shape, BF),
            pltpu.VMEM((GROUP, ROWS, wide), BF),
            pltpu.VMEM((GROUP, ROWS, wide), BF),
            block, block, mixed, block, block, mixed,
            block, block, mixed, block, block, mixed,
            pltpu.VMEM((ROWS, width), BF),
            pltpu.VMEM((ROWS, width), BF),
            pltpu.VMEM((GROUP, ROWS, wide), BF),
            pltpu.VMEM((GROUP, ROWS, wide), F32),
            pltpu.VMEM((GROUP, ROWS, hid), BF),
            pltpu.VMEM((4, 2, tokens), jnp.int32),
            pltpu.VMEM((tokens, width), BF), pltpu.VMEM((tokens, width), BF),
            pltpu.VMEM((tokens, width), BF), pltpu.VMEM((tokens, width), BF),
            sems((2,)), sems((2,)), sems((4,)),
            sems((GROUP, 2 + CHUNKS)), sems((GROUP, 2 + CHUNKS)),
            sems((3, EXPERTS)), sems((3, EXPERTS)), sems((3,)),
            sems((3 * CHUNKS, EXPERTS)), sems((3 * CHUNKS, EXPERTS)), sems((3 * CHUNKS,)),
            sems((2, CHUNKS)), sems((2, CHUNKS)), sems((4,)), sems((4,)),
        ],
        compiler_params=pltpu.CompilerParams(
            collective_id=0, has_side_effects=True, vmem_limit_bytes=60 * 1024 * 1024
        ),
    )(
        acts[0], grads[0], routes_f[0].T, gate_f[0].T, routes_b[0].T, gate_b[0].T,
        by_slot, gate_up[0, 0], down[0, 0],
    )
    moe_out, input_grad = pl.pallas_call(
        write_out,
        out_shape=(out, out),
        in_specs=[vmem, vmem],
        out_specs=(hbm, hbm),
        scratch_shapes=[sems((2,))],
    )(*results)
    return moe_out[None], input_grad[None]


def solution(mesh):
    three = P("pipe", "expert", None)
    four = P("pipe", "expert", None, None)
    return jax.shard_map(
        functools.partial(on_device, mesh.shape["pipe"]),
        mesh=mesh,
        in_specs=(three,) * 6 + (P("pipe", "expert", None, None, None), four, four),
        out_specs=(three, three),
        check_vma=False,
    )
```

```python
import functools

import jax
import jax.numpy as jnp
from jax import lax
from jax.experimental import pallas as pl
from jax.experimental.pallas import tpu as pltpu
from jax.sharding import PartitionSpec as P

MESH = pl.DeviceIdType.MESH
EXPERTS = 8
GROUP = 4
MAIN = 16
REST = 4
BF = jnp.bfloat16
F32 = jnp.float32
ROWS_MAIN = EXPERTS * MAIN
ROWS_MIX = EXPERTS * 2 * REST
ROWS = ROWS_MAIN + ROWS_MIX
PARTS = (768, 768, 640, 384)
CHUNKS = len(PARTS)
STEPS = 4
FOLDS = 4


def dot(a, b, ca=1, cb=0):
    return lax.dot_general(a, b, (((ca,), (cb,)), ((), ())), preferred_element_type=F32)


def places(routes, gates):
    tokens = routes.shape[1]
    names = [routes[k : k + 1, :] for k in range(2)]
    experts = lax.broadcasted_iota(jnp.int32, (EXPERTS, tokens), 0)
    onehot = [(name == experts).astype(F32) for name in names]
    row = lax.broadcasted_iota(jnp.int32, (tokens, tokens), 0)
    column = lax.broadcasted_iota(jnp.int32, (tokens, tokens), 1)
    before = dot((onehot[0] + onehot[1]).astype(BF), (row < column).astype(BF))
    sel = [jnp.zeros((rows, tokens), F32) for rows in (ROWS_MAIN, ROWS_MIX, ROWS_MIX)]
    at = [lax.broadcasted_iota(jnp.int32, s.shape, 0) for s in sel]
    comb = list(sel)
    for k in range(2):
        slot = jnp.sum(onehot[k] * before, axis=0, keepdims=True).astype(jnp.int32)
        gate = gates[k : k + 1, :].astype(F32) * (1.0 / 128.0)
        in_main = jnp.where(slot < MAIN, names[k] * MAIN + slot, -1)
        in_low = jnp.where(slot < MAIN, -1, names[k] * (2 * REST) + slot - MAIN)
        in_high = jnp.where(slot < MAIN, -1, in_low + REST)
        for i, place in enumerate((in_main, in_low, in_high)):
            hit = (at[i] == place).astype(F32)
            sel[i] = sel[i] + hit
            comb[i] = comb[i] + hit * gate
    return [s.astype(BF) for s in sel] + [c.T.astype(BF) for c in comb]


def kernel(
    n_pipe,
    acts, grads, routes_f, gate_f, routes_b, gate_b, saved, gate_up, down,
    moe_out, input_grad,
    x_in, g_in, w_gu, w_d, raw, sv_out, sv,
    s_f, s_b, s_m, r_f, r_b, r_m,
    y_f, y_b, y_m, h_f, h_b, e_f, e_b, k_f, k_b,
    x_f, x_b, pre_b, proj_f, hid_f,
    meta, o_f, o_b, fin_f, fin_b,
    pipe_s, pipe_r, loc, plane_s, plane_r, z_s, z_r, z_l, q_s, q_r, q_l, fin_s, fin_r, fin_l, meta_s, meta_r,
):
    width = acts.shape[1]
    hid = down.shape[0]
    step = width // STEPS
    pipe = lax.axis_index("pipe")
    me = lax.axis_index("expert")
    z = me // GROUP
    line = lax.rem(me, GROUP)
    core = 1 - 2 * lax.rem(me, 2)
    side = 2 - 4 * lax.rem(me // 2, 2)
    mates = {0: me, 1: me + core, 2: me + side, 3: me + core + side}
    nxt = {"pipe": lax.rem(pipe + 1, n_pipe), "expert": mates[2]}
    prv = {"pipe": lax.rem(pipe + n_pipe - 1, n_pipe), "expert": mates[2]}
    pair = {"expert": mates[2]}

    def along(d):
        return lax.rem(z + d, EXPERTS)

    order = (4, 3, 5, 2, 6, 1, 7)
    load_raw = pltpu.make_async_copy(saved, raw, loc.at[3])
    load_raw.start()
    own = [
        pltpu.make_async_copy(down, w_d.at[0], loc.at[0]),
        pltpu.make_async_copy(gate_up, w_gu.at[0], loc.at[1]),
    ]
    for copy in own:
        copy.start()
    partners = [nxt, prv] + [{"expert": mates[r]} for r in (1, 2, 3)]
    partners += [{"expert": along(d) * GROUP + line} for d in order]
    barrier = pltpu.get_barrier_semaphore()
    for partner in partners:
        pl.semaphore_signal(barrier, inc=1, device_id=partner, device_id_type=MESH)
    pl.semaphore_wait(barrier, len(partners))

    def remote(src, dst, ssem, rsem, to):
        return pltpu.make_async_remote_copy(
            src_ref=src, dst_ref=dst, send_sem=ssem, recv_sem=rsem, device_id=to, device_id_type=MESH
        )

    shift_f = remote(acts, x_in, pipe_s.at[0], pipe_r.at[0], nxt)
    shift_b = remote(grads, g_in, pipe_s.at[1], pipe_r.at[1], prv)
    tables = [
        remote(table, meta.at[k], meta_s.at[k], meta_r.at[k], pair)
        for k, table in enumerate((routes_f, gate_f, routes_b, gate_b))
    ]
    for copy in tables:
        copy.start()
    shift_b.start()
    shift_f.start()

    parts = [pl.ds(sum(PARTS[:i]), PARTS[i]) for i in range(CHUNKS)]

    def send_down(src, r, by):
        return remote(src, w_d.at[r], plane_s.at[r, 0], plane_r.at[r, 0], {"expert": mates[by]})

    def send_gu(src, r, by, i):
        at = 2 + i
        return remote(src.at[parts[i]], w_gu.at[r, parts[i]], plane_s.at[r, at], plane_r.at[r, at], {"expert": mates[by]})

    def saved_to(r):
        to = mates[r]
        return remote(sv_out.at[lax.rem(mates[r ^ 2], GROUP)], sv.at[r], plane_s.at[r, 1], plane_r.at[r, 1], {"expert": to})

    downs = {1: send_down(down, 1, 1), 2: send_down(down, 2, 2), 3: send_down(w_d.at[2], 3, 1)}
    gus = {1: [send_gu(gate_up, 1, 1, i) for i in range(CHUNKS)]}
    gus[2] = [send_gu(gate_up, 2, 2, i) for i in range(CHUNKS)]
    gus[3] = [send_gu(w_gu.at[2], 3, 1, i) for i in range(CHUNKS)]
    kept = {r: saved_to(r) for r in (1, 2, 3)}
    downs[2].start()
    downs[1].start()

    load_raw.wait()
    flat = raw[...].reshape(raw.shape[0] * raw.shape[1], raw.shape[2])
    row = lax.broadcasted_iota(jnp.int32, (ROWS, flat.shape[0]), 0)
    column = lax.broadcasted_iota(jnp.int32, (ROWS, flat.shape[0]), 1)
    late = row - ROWS_MAIN
    slot = jnp.where(late < 0, row & (MAIN - 1), MAIN + (late & (REST - 1)))
    plane = jnp.where(late < 0, row >> 4, late >> 3)
    base = slot * raw.shape[1] + plane * GROUP
    for number in range(GROUP):
        pick = (column == base + number).astype(BF)
        sv_out[number] = dot(pick, flat).astype(BF)
    keep_own = pltpu.make_async_copy(sv_out.at[lax.rem(mates[2], GROUP)], sv.at[0], loc.at[2])
    keep_own.start()
    for r in (2, 3, 1):
        kept[r].start()
    for i in range(CHUNKS):
        gus[2][i].start()
        gus[1][i].start()

    for copy in tables:
        copy.wait_recv()
    sel_f, mix_f, _, comb_f, *rest_f = places(meta[0], meta[1])
    sel_b, _, mix_b, comb_b, *rest_b = places(meta[2], meta[3])

    def columns(i):
        return pl.ds(pl.multiple_of(i * step, step), step)

    everything = pl.ds(0, width)

    def travel(src, dst, sems, b, d, at):
        ssem, rsem = sems
        there = along(d)
        return remote(
            src.at[there, :, at], dst.at[z, :, at], ssem.at[b, d], rsem.at[b, d], {"expert": there * GROUP + line}
        )

    def arrive(src, dst, sems, b, d, at):
        ssem, rsem = sems
        there = along(EXPERTS - d)
        return remote(
            src.at[there, :, at], dst.at[there, :, at], ssem.at[b, d], rsem.at[b, d], {"expert": there * GROUP + line}
        )

    def start_all(src, dst, sems, local_sem, b, at):
        for d in order:
            travel(src, dst, sems, b, d, at).start()
        pltpu.make_async_copy(src.at[z, :, at], dst.at[z, :, at], local_sem.at[b]).start()

    def recv_all(src, dst, sems, local_sem, b, at):
        for d in order[::-1]:
            arrive(src, dst, sems, b, d, at).wait_recv()
        pltpu.make_async_copy(src.at[z, :, at], dst.at[z, :, at], local_sem.at[b]).wait()

    def sent_all(src, dst, sems, b, at):
        for d in order:
            travel(src, dst, sems, b, d, at).wait_send()

    out_sems, back_sems = (z_s, z_r), (q_s, q_r)

    shift_b.wait_recv()

    @pl.loop(0, STEPS)
    def _(i):
        at = columns(i)
        s_b[:, :, at] = dot(sel_b, g_in[:, at]).astype(BF).reshape(EXPERTS, MAIN, step)

    start_all(s_b, r_b, out_sems, z_l, 1, everything)
    shift_f.wait_recv()

    @pl.loop(0, STEPS)
    def _(i):
        at = columns(i)
        both = dot(mix_f, x_in[:, at]) + dot(mix_b, g_in[:, at])
        s_m[:, :, at] = both.reshape(EXPERTS, 2 * REST, step).astype(BF)

    start_all(s_m, r_m, out_sems, z_l, 2, everything)

    @pl.loop(0, STEPS)
    def _(i):
        at = columns(i)
        s_f[:, :, at] = dot(sel_f, x_in[:, at]).astype(BF).reshape(EXPERTS, MAIN, step)

    start_all(s_f, r_f, out_sems, z_l, 0, everything)

    for copy in own:
        copy.wait()
    keep_own.wait()
    downs[2].wait_recv()
    downs[3].start()
    recv_all(s_b, r_b, out_sems, z_l, 1, everything)
    x_b[:ROWS_MAIN, :] = r_b[...].reshape(ROWS_MAIN, width)
    recv_all(s_m, r_m, out_sems, z_l, 2, everything)
    mixed = r_m[...].reshape(ROWS_MIX, width)
    row = lax.broadcasted_iota(jnp.int32, (ROWS_MIX, ROWS_MIX), 0)
    column = lax.broadcasted_iota(jnp.int32, (ROWS_MIX, ROWS_MIX), 1)
    low = (row >> 3) * (2 * REST) + (row & (REST - 1))
    x_b[ROWS_MAIN:, :] = dot((column == low + REST).astype(BF), mixed).astype(BF)
    x_f[ROWS_MAIN:, :] = dot((column == low).astype(BF), mixed).astype(BF)
    for r in range(GROUP):
        if r in (1, 3):
            downs[r].wait_recv()
        if r:
            kept[r].wait_recv()
        back_hidden = dot(x_b[...], w_d[r], 1, 1)
        pre = sv[r].astype(F32)
        g, u = pre[:, :hid], pre[:, hid:]
        sigma = 1.0 / (1.0 + jnp.exp(-g))
        pre_b[r] = jnp.concatenate(
            [back_hidden * u * sigma * (1.0 + g * (1.0 - sigma)), back_hidden * g * sigma], axis=1
        ).astype(BF)

    def backward(i):
        at = parts[i]
        gus[2][i].wait_recv()
        gus[3][i].start()
        gus[1][i].wait_recv()
        total = dot(pre_b[0], w_gu[0, at, :], 1, 1)
        total = total + dot(pre_b[1], w_gu[1, at, :], 1, 1)
        total = total + dot(pre_b[2], w_gu[2, at, :], 1, 1)
        gus[3][i].wait_recv()
        total = total + dot(pre_b[3], w_gu[3, at, :], 1, 1)
        y_b[:, :, at] = total[:ROWS_MAIN].astype(BF).reshape(EXPERTS, MAIN, PARTS[i])
        y_m[:, :, at] = total[ROWS_MAIN:].astype(BF).reshape(EXPERTS, 2 * REST, PARTS[i])
        start_all(y_b, h_b, back_sems, q_l, 2 * CHUNKS + i, at)

    def fold(dst, start, size):
        shape = (ROWS_MIX, size)
        upper = (lax.broadcasted_iota(jnp.int32, shape, 0) & (2 * REST - 1)) < REST
        left = y_m[:, :, pl.ds(start, size)].reshape(shape).astype(F32)
        right = y_m[:, :, pl.ds(width // 2 + start, size)].reshape(shape).astype(F32)
        both = jnp.where(upper, left, right)
        dst[:, :, pl.ds(start, size)] = both.reshape(EXPERTS, 2 * REST, size).astype(BF)

    def project(i):
        at = parts[i]
        for r in range(GROUP):
            part = dot(x_f[:, at], w_gu[r, at, :])
            proj_f[r] = part if i == 0 else proj_f[r] + part

    for i in range(CHUNKS):
        backward(i)
        if i == CHUNKS - 1:
            fold(e_b, 0, width // 2)
            start_all(e_b, k_b, back_sems, q_l, FOLDS, pl.ds(0, width // 2))
        if i == 1:
            recv_all(s_f, r_f, out_sems, z_l, 0, everything)
            x_f[:ROWS_MAIN, :] = r_f[...].reshape(ROWS_MAIN, width)
            project(0)
        if i:
            project(i)
    for r in range(GROUP):
        a, b = proj_f[r, :, :hid], proj_f[r, :, hid:]
        hid_f[r] = (a * (1.0 / (1.0 + jnp.exp(-a))) * b).astype(BF)
    quarter = width // STEPS
    slabs = [pl.ds(i * quarter, quarter) for i in range(STEPS)]
    for i in range(STEPS):
        at = slabs[i]
        total = dot(hid_f[0], w_d[0, :, at])
        for r in range(1, GROUP):
            total = total + dot(hid_f[r], w_d[r, :, at])
        y_f[:, :, at] = total[:ROWS_MAIN].astype(BF).reshape(EXPERTS, MAIN, quarter)
        y_m[:, :, at] = total[ROWS_MAIN:].astype(BF).reshape(EXPERTS, 2 * REST, quarter)
        start_all(y_f, h_f, back_sems, q_l, i, at)
        if i >= 2:
            fold(e_f, (i - 2) * quarter, quarter)
            start_all(e_f, k_f, back_sems, q_l, FOLDS + i - 1, slabs[i - 2])

    def finished(which, i):
        src, dst = ((o_f, fin_f), (o_b, fin_b))[which]
        return remote(src.at[:, slabs[i]], dst.at[:, slabs[i]], fin_s.at[which, i], fin_r.at[which, i], pair)

    def finish(which, i):
        at = slabs[i]
        own_in, main, further, comb, rest, out = (
            (x_in, h_f, k_f, comb_f, rest_f, o_f),
            (g_in, h_b, k_b, comb_b, rest_b, o_b),
        )[which]
        total = own_in[:, at].astype(F32) + dot(comb, main[:, :, at].reshape(ROWS_MAIN, quarter))
        total = total + dot(rest[i // 2], further[:, :, slabs[i % 2]].reshape(ROWS_MIX, quarter))
        out[:, at] = total.astype(BF)
        finished(which, i).start()

    def leave(which, i):
        src, dst = ((fin_f, moe_out), (fin_b, input_grad))[which]
        return pltpu.make_async_copy(src.at[:, slabs[i]], dst.at[:, slabs[i]], fin_l.at[which, i])

    for i in range(CHUNKS):
        recv_all(y_b, h_b, back_sems, q_l, 2 * CHUNKS + i, parts[i])
    recv_all(e_b, k_b, back_sems, q_l, FOLDS, pl.ds(0, width // 2))
    for i in range(STEPS):
        finish(1, i)
    for i in range(STEPS):
        finished(1, i).wait_recv()
        leave(1, i).start()
    for i in (0, 2, 1, 3):
        if i == 0:
            for k in range(3):
                recv_all(y_f, h_f, back_sems, q_l, k, slabs[k])
            recv_all(e_f, k_f, back_sems, q_l, FOLDS + 1, slabs[0])
        if i == 1:
            recv_all(y_f, h_f, back_sems, q_l, 3, slabs[3])
            recv_all(e_f, k_f, back_sems, q_l, FOLDS + 2, slabs[1])
        finish(0, i)
    for i in (0, 2, 1, 3):
        finished(0, i).wait_recv()
        leave(0, i).start()

    for copy in tables:
        copy.wait_send()
    for i in range(STEPS):
        for which in (0, 1):
            finished(which, i).wait_send()
            leave(which, i).wait()
    for src, dst, b in ((s_f, r_f, 0), (s_b, r_b, 1), (s_m, r_m, 2)):
        sent_all(src, dst, out_sems, b, everything)
    for i in range(CHUNKS):
        sent_all(y_b, h_b, back_sems, 2 * CHUNKS + i, parts[i])
    for i in range(STEPS):
        sent_all(y_f, h_f, back_sems, i, slabs[i])
    sent_all(e_b, k_b, back_sems, FOLDS, pl.ds(0, width // 2))
    for i in range(2):
        sent_all(e_f, k_f, back_sems, FOLDS + 1 + i, slabs[i])
    shift_f.wait_send()
    shift_b.wait_send()
    for r in (1, 2, 3):
        downs[r].wait_send()
        kept[r].wait_send()
        for copy in gus[r]:
            copy.wait_send()


def write_out(a, b, out_a, out_b, sem):
    copies = [pltpu.make_async_copy(a, out_a, sem.at[0]), pltpu.make_async_copy(b, out_b, sem.at[1])]
    for copy in copies:
        copy.start()
    for copy in copies:
        copy.wait()


def on_device(n_pipe, acts, grads, routes_f, gate_f, routes_b, gate_b, saved, gate_up, down):
    tokens, width = acts.shape[1:]
    hid = down.shape[2]
    wide = gate_up.shape[3]
    vmem = pl.BlockSpec(memory_space=pltpu.VMEM)
    hbm = pl.BlockSpec(memory_space=pl.ANY)
    block = pltpu.VMEM((EXPERTS, MAIN, width), BF)
    mixed = pltpu.VMEM((EXPERTS, 2 * REST, width), BF)
    folded = pltpu.VMEM((EXPERTS, 2 * REST, width // 2), BF)
    sems = pltpu.SemaphoreType.DMA
    out = jax.ShapeDtypeStruct((tokens, width), BF)
    by_slot = saved[0, 0].transpose(1, 0, 2)
    results = pl.pallas_call(
        functools.partial(kernel, n_pipe),
        out_shape=(out, out),
        in_specs=[hbm, hbm, vmem, vmem, vmem, vmem, hbm, hbm, hbm],
        out_specs=(hbm, hbm),
        scratch_shapes=[
            pltpu.VMEM((tokens, width), BF),
            pltpu.VMEM((tokens, width), BF),
            pltpu.VMEM((GROUP, width, wide), BF),
            pltpu.VMEM((GROUP, hid, width), BF),
            pltpu.VMEM(by_slot.shape, BF),
            pltpu.VMEM((GROUP, ROWS, wide), BF),
            pltpu.VMEM((GROUP, ROWS, wide), BF),
            block, block, mixed, block, block, mixed,
            block, block, mixed, block, block, folded, folded, folded, folded,
            pltpu.VMEM((ROWS, width), BF),
            pltpu.VMEM((ROWS, width), BF),
            pltpu.VMEM((GROUP, ROWS, wide), BF),
            pltpu.VMEM((GROUP, ROWS, wide), F32),
            pltpu.VMEM((GROUP, ROWS, hid), BF),
            pltpu.VMEM((4, 2, tokens), jnp.int32),
            pltpu.VMEM((tokens, width), BF), pltpu.VMEM((tokens, width), BF),
            pltpu.VMEM((tokens, width), BF), pltpu.VMEM((tokens, width), BF),
            sems((2,)), sems((2,)), sems((4,)),
            sems((GROUP, 2 + CHUNKS)), sems((GROUP, 2 + CHUNKS)),
            sems((3, EXPERTS)), sems((3, EXPERTS)), sems((3,)),
            sems((3 * CHUNKS, EXPERTS)), sems((3 * CHUNKS, EXPERTS)), sems((3 * CHUNKS,)),
            sems((2, STEPS)), sems((2, STEPS)), sems((2, STEPS)), sems((4,)), sems((4,)),
        ],
        compiler_params=pltpu.CompilerParams(
            collective_id=0, has_side_effects=True, vmem_limit_bytes=60 * 1024 * 1024
        ),
    )(
        acts[0], grads[0], routes_f[0].T, gate_f[0].T, routes_b[0].T, gate_b[0].T,
        by_slot, gate_up[0, 0], down[0, 0],
    )
    moe_out, input_grad = pl.pallas_call(
        write_out,
        out_shape=(out, out),
        in_specs=[vmem, vmem],
        out_specs=(hbm, hbm),
        scratch_shapes=[sems((2,))],
    )(*results)
    return moe_out[None], input_grad[None]


def solution(mesh):
    three = P("pipe", "expert", None)
    four = P("pipe", "expert", None, None)
    return jax.shard_map(
        functools.partial(on_device, mesh.shape["pipe"]),
        mesh=mesh,
        in_specs=(three,) * 6 + (P("pipe", "expert", None, None, None), four, four),
        out_specs=(three, three),
        check_vma=False,
    )
```

```python
import functools

import jax
import jax.numpy as jnp
from jax import lax
from jax.experimental import pallas as pl
from jax.experimental.pallas import tpu as pltpu
from jax.sharding import PartitionSpec as P

MESH = pl.DeviceIdType.MESH
EXPERTS = 8
GROUP = 4
MAIN = 16
REST = 4
BF = jnp.bfloat16
F32 = jnp.float32
ROWS_MAIN = EXPERTS * MAIN
ROWS_MIX = EXPERTS * 2 * REST
ROWS = ROWS_MAIN + ROWS_MIX
PARTS = (896, 896, 512, 256)
CHUNKS = len(PARTS)
STEPS = 4
FOLDS = 4


def dot(a, b, ca=1, cb=0):
    return lax.dot_general(a, b, (((ca,), (cb,)), ((), ())), preferred_element_type=F32)


def places(routes, gates):
    tokens = routes.shape[1]
    names = [routes[k : k + 1, :] for k in range(2)]
    experts = lax.broadcasted_iota(jnp.int32, (EXPERTS, tokens), 0)
    onehot = [(name == experts).astype(F32) for name in names]
    row = lax.broadcasted_iota(jnp.int32, (tokens, tokens), 0)
    column = lax.broadcasted_iota(jnp.int32, (tokens, tokens), 1)
    before = dot((onehot[0] + onehot[1]).astype(BF), (row < column).astype(BF))
    sel = [jnp.zeros((rows, tokens), F32) for rows in (ROWS_MAIN, ROWS_MIX, ROWS_MIX)]
    at = [lax.broadcasted_iota(jnp.int32, s.shape, 0) for s in sel]
    comb = list(sel)
    for k in range(2):
        slot = jnp.sum(onehot[k] * before, axis=0, keepdims=True).astype(jnp.int32)
        gate = gates[k : k + 1, :].astype(F32) * (1.0 / 128.0)
        in_main = jnp.where(slot < MAIN, names[k] * MAIN + slot, -1)
        in_low = jnp.where(slot < MAIN, -1, names[k] * (2 * REST) + slot - MAIN)
        in_high = jnp.where(slot < MAIN, -1, in_low + REST)
        for i, place in enumerate((in_main, in_low, in_high)):
            hit = (at[i] == place).astype(F32)
            sel[i] = sel[i] + hit
            comb[i] = comb[i] + hit * gate
    return [s.astype(BF) for s in sel] + [c.T.astype(BF) for c in comb]


def kernel(
    n_pipe,
    acts, grads, routes_f, gate_f, routes_b, gate_b, saved, gate_up, down,
    moe_out, input_grad,
    x_in, g_in, w_gu, w_d, raw, sv_out, sv,
    s_f, s_b, s_m, r_f, r_b, r_m,
    y_f, y_b, y_m, h_f, h_b, e_f, e_b, k_f, k_b,
    x_f, x_b, pre_b, proj_f, hid_f,
    meta, o_f, o_b, fin_f, fin_b,
    pipe_s, pipe_r, loc, plane_s, plane_r, z_s, z_r, z_l, q_s, q_r, q_l, fin_s, fin_r, fin_l, meta_s, meta_r,
):
    width = acts.shape[1]
    hid = down.shape[0]
    step = width // STEPS
    pipe = lax.axis_index("pipe")
    me = lax.axis_index("expert")
    z = me // GROUP
    line = lax.rem(me, GROUP)
    core = 1 - 2 * lax.rem(me, 2)
    side = 2 - 4 * lax.rem(me // 2, 2)
    mates = {0: me, 1: me + core, 2: me + side, 3: me + core + side}
    nxt = {"pipe": lax.rem(pipe + 1, n_pipe), "expert": mates[2]}
    prv = {"pipe": lax.rem(pipe + n_pipe - 1, n_pipe), "expert": mates[2]}
    pair = {"expert": mates[2]}

    def along(d):
        return lax.rem(z + d, EXPERTS)

    order = (4, 3, 5, 2, 6, 1, 7)
    load_raw = pltpu.make_async_copy(saved, raw, loc.at[3])
    load_raw.start()
    own = [
        pltpu.make_async_copy(down, w_d.at[0], loc.at[0]),
        pltpu.make_async_copy(gate_up, w_gu.at[0], loc.at[1]),
    ]
    for copy in own:
        copy.start()
    partners = [nxt, prv] + [{"expert": mates[r]} for r in (1, 2, 3)]
    partners += [{"expert": along(d) * GROUP + line} for d in order]
    barrier = pltpu.get_barrier_semaphore()
    for partner in partners:
        pl.semaphore_signal(barrier, inc=1, device_id=partner, device_id_type=MESH)
    pl.semaphore_wait(barrier, len(partners))

    def remote(src, dst, ssem, rsem, to):
        return pltpu.make_async_remote_copy(
            src_ref=src, dst_ref=dst, send_sem=ssem, recv_sem=rsem, device_id=to, device_id_type=MESH
        )

    slabs = [pl.ds(i * step, step) for i in range(STEPS)]
    shift_f = remote(acts, x_in, pipe_s.at[STEPS], pipe_r.at[STEPS], nxt)
    shift_b = [
        remote(grads.at[:, slabs[i]], g_in.at[:, slabs[i]], pipe_s.at[i], pipe_r.at[i], prv) for i in range(STEPS)
    ]
    tables = [
        remote(table, meta.at[k], meta_s.at[k], meta_r.at[k], pair)
        for k, table in enumerate((routes_f, gate_f, routes_b, gate_b))
    ]
    for copy in tables:
        copy.start()
    for copy in shift_b:
        copy.start()
    shift_f.start()

    parts = [pl.ds(sum(PARTS[:i]), PARTS[i]) for i in range(CHUNKS)]

    def send_down(src, r, by):
        return remote(src, w_d.at[r], plane_s.at[r, 0], plane_r.at[r, 0], {"expert": mates[by]})

    def send_gu(src, r, by, i):
        at = 2 + i
        return remote(src.at[parts[i]], w_gu.at[r, parts[i]], plane_s.at[r, at], plane_r.at[r, at], {"expert": mates[by]})

    def saved_to(r):
        to = mates[r]
        return remote(sv_out.at[lax.rem(mates[r ^ 2], GROUP)], sv.at[r], plane_s.at[r, 1], plane_r.at[r, 1], {"expert": to})

    downs = {1: send_down(down, 1, 1), 2: send_down(down, 2, 2), 3: send_down(w_d.at[2], 3, 1)}
    gus = {1: [send_gu(gate_up, 1, 1, i) for i in range(CHUNKS)]}
    gus[2] = [send_gu(gate_up, 2, 2, i) for i in range(CHUNKS)]
    gus[3] = [send_gu(w_gu.at[2], 3, 1, i) for i in range(CHUNKS)]
    kept = {r: saved_to(r) for r in (1, 2, 3)}
    downs[2].start()
    downs[1].start()

    for copy in tables:
        copy.wait_recv()
    sel_f, mix_f, _, comb_f, *rest_f = places(meta[0], meta[1])
    sel_b, _, mix_b, comb_b, *rest_b = places(meta[2], meta[3])

    def columns(i):
        return pl.ds(pl.multiple_of(i * step, step), step)

    everything = pl.ds(0, width)

    def travel(src, dst, sems, b, d, at):
        ssem, rsem = sems
        there = along(d)
        return remote(
            src.at[there, :, at], dst.at[z, :, at], ssem.at[b, d], rsem.at[b, d], {"expert": there * GROUP + line}
        )

    def arrive(src, dst, sems, b, d, at):
        ssem, rsem = sems
        there = along(EXPERTS - d)
        return remote(
            src.at[there, :, at], dst.at[there, :, at], ssem.at[b, d], rsem.at[b, d], {"expert": there * GROUP + line}
        )

    def start_all(src, dst, sems, local_sem, b, at):
        for d in order:
            travel(src, dst, sems, b, d, at).start()
        pltpu.make_async_copy(src.at[z, :, at], dst.at[z, :, at], local_sem.at[b]).start()

    def recv_all(src, dst, sems, local_sem, b, at):
        for d in order[::-1]:
            arrive(src, dst, sems, b, d, at).wait_recv()
        pltpu.make_async_copy(src.at[z, :, at], dst.at[z, :, at], local_sem.at[b]).wait()

    def sent_all(src, dst, sems, b, at):
        for d in order:
            travel(src, dst, sems, b, d, at).wait_send()

    out_sems, back_sems = (z_s, z_r), (q_s, q_r)

    for i, at in enumerate(slabs):
        shift_b[i].wait_recv()
        s_b[:, :, at] = dot(sel_b, g_in[:, at]).astype(BF).reshape(EXPERTS, MAIN, step)
        start_all(s_b, r_b, out_sems, z_l, 2 + i, at)
    shift_f.wait_recv()

    @pl.loop(0, STEPS)
    def _(i):
        at = columns(i)
        both = dot(mix_f, x_in[:, at]) + dot(mix_b, g_in[:, at])
        s_m[:, :, at] = both.reshape(EXPERTS, 2 * REST, step).astype(BF)

    start_all(s_m, r_m, out_sems, z_l, 1, everything)

    @pl.loop(0, STEPS)
    def _(i):
        at = columns(i)
        s_f[:, :, at] = dot(sel_f, x_in[:, at]).astype(BF).reshape(EXPERTS, MAIN, step)

    start_all(s_f, r_f, out_sems, z_l, 0, everything)

    load_raw.wait()
    flat = raw[...].reshape(raw.shape[0] * raw.shape[1], raw.shape[2])
    row = lax.broadcasted_iota(jnp.int32, (ROWS, flat.shape[0]), 0)
    column = lax.broadcasted_iota(jnp.int32, (ROWS, flat.shape[0]), 1)
    late = row - ROWS_MAIN
    slot = jnp.where(late < 0, row & (MAIN - 1), MAIN + (late & (REST - 1)))
    plane = jnp.where(late < 0, row >> 4, late >> 3)
    base = slot * raw.shape[1] + plane * GROUP
    for number in range(GROUP):
        pick = (column == base + number).astype(BF)
        sv_out[number] = dot(pick, flat).astype(BF)
    keep_own = pltpu.make_async_copy(sv_out.at[lax.rem(mates[2], GROUP)], sv.at[0], loc.at[2])
    keep_own.start()
    for r in (2, 3, 1):
        kept[r].start()
    for i in range(CHUNKS):
        gus[2][i].start()
        gus[1][i].start()

    for copy in own:
        copy.wait()
    keep_own.wait()
    downs[2].wait_recv()
    downs[3].start()
    for i, at in enumerate(slabs):
        recv_all(s_b, r_b, out_sems, z_l, 2 + i, at)
    x_b[:ROWS_MAIN, :] = r_b[...].reshape(ROWS_MAIN, width)
    recv_all(s_m, r_m, out_sems, z_l, 1, everything)
    mixed = r_m[...].reshape(ROWS_MIX, width)
    row = lax.broadcasted_iota(jnp.int32, (ROWS_MIX, ROWS_MIX), 0)
    column = lax.broadcasted_iota(jnp.int32, (ROWS_MIX, ROWS_MIX), 1)
    low = (row >> 3) * (2 * REST) + (row & (REST - 1))
    x_b[ROWS_MAIN:, :] = dot((column == low + REST).astype(BF), mixed).astype(BF)
    x_f[ROWS_MAIN:, :] = dot((column == low).astype(BF), mixed).astype(BF)
    for r in range(GROUP):
        if r in (1, 3):
            downs[r].wait_recv()
        if r:
            kept[r].wait_recv()
        back_hidden = dot(x_b[...], w_d[r], 1, 1)
        pre = sv[r].astype(F32)
        g, u = pre[:, :hid], pre[:, hid:]
        sigma = 1.0 / (1.0 + jnp.exp(-g))
        pre_b[r] = jnp.concatenate(
            [back_hidden * u * sigma * (1.0 + g * (1.0 - sigma)), back_hidden * g * sigma], axis=1
        ).astype(BF)

    def backward(i):
        at = parts[i]
        gus[2][i].wait_recv()
        gus[3][i].start()
        gus[1][i].wait_recv()
        total = dot(pre_b[0], w_gu[0, at, :], 1, 1)
        total = total + dot(pre_b[1], w_gu[1, at, :], 1, 1)
        total = total + dot(pre_b[2], w_gu[2, at, :], 1, 1)
        gus[3][i].wait_recv()
        total = total + dot(pre_b[3], w_gu[3, at, :], 1, 1)
        y_b[:, :, at] = total[:ROWS_MAIN].astype(BF).reshape(EXPERTS, MAIN, PARTS[i])
        y_m[:, :, at] = total[ROWS_MAIN:].astype(BF).reshape(EXPERTS, 2 * REST, PARTS[i])
        start_all(y_b, h_b, back_sems, q_l, 2 * CHUNKS + i, at)

    def fold(dst, start, size):
        shape = (ROWS_MIX, size)
        upper = (lax.broadcasted_iota(jnp.int32, shape, 0) & (2 * REST - 1)) < REST
        left = y_m[:, :, pl.ds(start, size)].reshape(shape).astype(F32)
        right = y_m[:, :, pl.ds(width // 2 + start, size)].reshape(shape).astype(F32)
        both = jnp.where(upper, left, right)
        dst[:, :, pl.ds(start, size)] = both.reshape(EXPERTS, 2 * REST, size).astype(BF)

    last = PARTS[-1]
    folds = ((0, width // 2 - last), (width // 2 - last, last))

    def project(i):
        at = parts[i]
        for r in range(GROUP):
            part = dot(x_f[:, at], w_gu[r, at, :])
            proj_f[r] = part if i == 0 else proj_f[r] + part

    for i in range(CHUNKS):
        backward(i)
        if i >= CHUNKS - 2:
            start, size = folds[i - CHUNKS + 2]
            fold(e_b, start, size)
            start_all(e_b, k_b, back_sems, q_l, FOLDS + 3 * (i - CHUNKS + 2), pl.ds(start, size))
        if i == 1:
            recv_all(s_f, r_f, out_sems, z_l, 0, everything)
            x_f[:ROWS_MAIN, :] = r_f[...].reshape(ROWS_MAIN, width)
            project(0)
        if i:
            project(i)
    for r in range(GROUP):
        a, b = proj_f[r, :, :hid], proj_f[r, :, hid:]
        hid_f[r] = (a * (1.0 / (1.0 + jnp.exp(-a))) * b).astype(BF)
    for i in range(STEPS):
        at = slabs[i]
        total = dot(hid_f[0], w_d[0, :, at])
        for r in range(1, GROUP):
            total = total + dot(hid_f[r], w_d[r, :, at])
        y_f[:, :, at] = total[:ROWS_MAIN].astype(BF).reshape(EXPERTS, MAIN, step)
        y_m[:, :, at] = total[ROWS_MAIN:].astype(BF).reshape(EXPERTS, 2 * REST, step)
        start_all(y_f, h_f, back_sems, q_l, i, at)
        if i >= 2:
            fold(e_f, (i - 2) * step, step)
            start_all(e_f, k_f, back_sems, q_l, FOLDS + i - 1, slabs[i - 2])

    def finished(which, i):
        src, dst = ((o_f, fin_f), (o_b, fin_b))[which]
        return remote(src.at[:, slabs[i]], dst.at[:, slabs[i]], fin_s.at[which, i], fin_r.at[which, i], pair)

    def finish(which, i):
        at = slabs[i]
        own_in, main, further, comb, rest, out = (
            (x_in, h_f, k_f, comb_f, rest_f, o_f),
            (g_in, h_b, k_b, comb_b, rest_b, o_b),
        )[which]
        total = own_in[:, at].astype(F32) + dot(comb, main[:, :, at].reshape(ROWS_MAIN, step))
        total = total + dot(rest[i // 2], further[:, :, slabs[i % 2]].reshape(ROWS_MIX, step))
        out[:, at] = total.astype(BF)
        finished(which, i).start()

    def leave(which, i):
        src, dst = ((fin_f, moe_out), (fin_b, input_grad))[which]
        return pltpu.make_async_copy(src.at[:, slabs[i]], dst.at[:, slabs[i]], fin_l.at[which, i])

    for i in range(CHUNKS):
        recv_all(y_b, h_b, back_sems, q_l, 2 * CHUNKS + i, parts[i])
    for i in range(2):
        recv_all(e_b, k_b, back_sems, q_l, FOLDS + 3 * i, pl.ds(*folds[i]))
    for i in range(STEPS):
        finish(1, i)
    for i in range(STEPS):
        finished(1, i).wait_recv()
        leave(1, i).start()
    for i in (0, 2, 1, 3):
        if i == 0:
            for k in range(3):
                recv_all(y_f, h_f, back_sems, q_l, k, slabs[k])
            recv_all(e_f, k_f, back_sems, q_l, FOLDS + 1, slabs[0])
        if i == 1:
            recv_all(y_f, h_f, back_sems, q_l, 3, slabs[3])
            recv_all(e_f, k_f, back_sems, q_l, FOLDS + 2, slabs[1])
        finish(0, i)
    for i in (0, 2, 1, 3):
        finished(0, i).wait_recv()
        leave(0, i).start()

    for copy in tables:
        copy.wait_send()
    for i in range(STEPS):
        for which in (0, 1):
            finished(which, i).wait_send()
            leave(which, i).wait()
    for src, dst, b in ((s_f, r_f, 0), (s_m, r_m, 1)):
        sent_all(src, dst, out_sems, b, everything)
    for i, at in enumerate(slabs):
        sent_all(s_b, r_b, out_sems, 2 + i, at)
    for i in range(CHUNKS):
        sent_all(y_b, h_b, back_sems, 2 * CHUNKS + i, parts[i])
    for i in range(STEPS):
        sent_all(y_f, h_f, back_sems, i, slabs[i])
    for i in range(2):
        sent_all(e_f, k_f, back_sems, FOLDS + 1 + i, slabs[i])
        sent_all(e_b, k_b, back_sems, FOLDS + 3 * i, pl.ds(*folds[i]))
    shift_f.wait_send()
    for copy in shift_b:
        copy.wait_send()
    for r in (1, 2, 3):
        downs[r].wait_send()
        kept[r].wait_send()
        for copy in gus[r]:
            copy.wait_send()


def write_out(a, b, out_a, out_b, sem):
    copies = [pltpu.make_async_copy(a, out_a, sem.at[0]), pltpu.make_async_copy(b, out_b, sem.at[1])]
    for copy in copies:
        copy.start()
    for copy in copies:
        copy.wait()


def on_device(n_pipe, acts, grads, routes_f, gate_f, routes_b, gate_b, saved, gate_up, down):
    tokens, width = acts.shape[1:]
    hid = down.shape[2]
    wide = gate_up.shape[3]
    vmem = pl.BlockSpec(memory_space=pltpu.VMEM)
    hbm = pl.BlockSpec(memory_space=pl.ANY)
    block = pltpu.VMEM((EXPERTS, MAIN, width), BF)
    mixed = pltpu.VMEM((EXPERTS, 2 * REST, width), BF)
    folded = pltpu.VMEM((EXPERTS, 2 * REST, width // 2), BF)
    sems = pltpu.SemaphoreType.DMA
    out = jax.ShapeDtypeStruct((tokens, width), BF)
    by_slot = saved[0, 0].transpose(1, 0, 2)
    results = pl.pallas_call(
        functools.partial(kernel, n_pipe),
        out_shape=(out, out),
        in_specs=[hbm, hbm, vmem, vmem, vmem, vmem, hbm, hbm, hbm],
        out_specs=(hbm, hbm),
        scratch_shapes=[
            pltpu.VMEM((tokens, width), BF),
            pltpu.VMEM((tokens, width), BF),
            pltpu.VMEM((GROUP, width, wide), BF),
            pltpu.VMEM((GROUP, hid, width), BF),
            pltpu.VMEM(by_slot.shape, BF),
            pltpu.VMEM((GROUP, ROWS, wide), BF),
            pltpu.VMEM((GROUP, ROWS, wide), BF),
            block, block, mixed, block, block, mixed,
            block, block, mixed, block, block, folded, folded, folded, folded,
            pltpu.VMEM((ROWS, width), BF),
            pltpu.VMEM((ROWS, width), BF),
            pltpu.VMEM((GROUP, ROWS, wide), BF),
            pltpu.VMEM((GROUP, ROWS, wide), F32),
            pltpu.VMEM((GROUP, ROWS, hid), BF),
            pltpu.VMEM((4, 2, tokens), jnp.int32),
            pltpu.VMEM((tokens, width), BF), pltpu.VMEM((tokens, width), BF),
            pltpu.VMEM((tokens, width), BF), pltpu.VMEM((tokens, width), BF),
            sems((STEPS + 1,)), sems((STEPS + 1,)), sems((4,)),
            sems((GROUP, 2 + CHUNKS)), sems((GROUP, 2 + CHUNKS)),
            sems((2 + STEPS, EXPERTS)), sems((2 + STEPS, EXPERTS)), sems((2 + STEPS,)),
            sems((3 * CHUNKS, EXPERTS)), sems((3 * CHUNKS, EXPERTS)), sems((3 * CHUNKS,)),
            sems((2, STEPS)), sems((2, STEPS)), sems((2, STEPS)), sems((4,)), sems((4,)),
        ],
        compiler_params=pltpu.CompilerParams(
            collective_id=0, has_side_effects=True, vmem_limit_bytes=60 * 1024 * 1024
        ),
    )(
        acts[0], grads[0], routes_f[0].T, gate_f[0].T, routes_b[0].T, gate_b[0].T,
        by_slot, gate_up[0, 0], down[0, 0],
    )
    moe_out, input_grad = pl.pallas_call(
        write_out,
        out_shape=(out, out),
        in_specs=[vmem, vmem],
        out_specs=(hbm, hbm),
        scratch_shapes=[sems((2,))],
    )(*results)
    return moe_out[None], input_grad[None]


def solution(mesh):
    three = P("pipe", "expert", None)
    four = P("pipe", "expert", None, None)
    return jax.shard_map(
        functools.partial(on_device, mesh.shape["pipe"]),
        mesh=mesh,
        in_specs=(three,) * 6 + (P("pipe", "expert", None, None, None), four, four),
        out_specs=(three, three),
        check_vma=False,
    )
```
